32 devices in a mesh: shot: 2 (over x), tile: 16 (over z, y, core).
Axes of the slice: x: 2, y: 2, z: 4, core: 2. Of those that a mesh axis runs over, the one named last changes fastest.
Arguments:
- wave_now: float32 [4, 32, 32, 128], P('shot', 'tile'), parts along dimension 0, may hold values from -6 to 6
- wave_prev: float32 [4, 32, 32, 128], P('shot', 'tile'), parts along dimension 0, may hold values from -6 to 6
- facies: int32 [32, 32, 128], P('tile'), may hold values from 0 to 7
- velocity_table: float32 [8], replicated, may hold values from 0.05 to 0.2
- epsilon_table: float32 [8], replicated, may hold values from 0 to 0.2
- tilt_table: float32 [8], replicated, may hold values from -0.6 to 0.6
- source_cell: int32 [2], P('shot'), parts along dimension 0, may hold values from 0 to 4095
- source_wavelet: float32 [8], P('shot'), parts along dimension 0, may hold values from -8 to 8
- receiver_cells: int32 [4096], P('shot'), parts along dimension 0, may hold values from 0 to 4095
- receiver_data: float32 [4, 4096], P(None, 'shot'), parts along dimension 1, may hold values from -6 to 6
Outputs:
- filtered: bfloat16 [64, 32, 32, 128], P('shot', None, 'tile'), parts along dimension 0
- wave_out: float32 [4, 32, 32, 128], P('shot', 'tile'), parts along dimension 0
The draws below stay inside these ranges and needn't reach their ends.
There are 2 independent parts, one for each index of `shot`. The reference program is written for one: setup_inputs(seed, part) draws one part's arguments, and reference() takes and returns one part's arrays. A program takes and returns all parts, laid end to end along the dimension named above; an argument that names none is the same for every part. Nothing has to cross between parts.
Inputs may be any that keep to these rules, and one draw needn't show every extreme that they name: `source_cell`: a surface cell y * 128 + x. `receiver_cells`: surface cells y * 128 + x; cells may repeat.
All inputs are finite; a program needn't handle non-finite values.
Results may differ from the reference program's by a relative error of at most 0.001.
The reference program's roundings to bfloat16 on the way (of `snapshot` and `image`) count: a program that leaves them out, or rounds other values in their place, can miss the bound.
Values may be sent and summed in bfloat16 or wider, within the bound.
A program may use at most 64 MiB of HBM per device.

```python
import jax
import jax.numpy as jnp
from jax import lax

NX = 128
NREC = 2048
NLAG = 32
STEPS = 4
NFAC = 8
NY = 32
NZ = 32


def touch_ends(entries, key, smallest, largest):
    dims = entries.shape
    index_at = [jax.random.randint(jax.random.fold_in(key, axis), (), 0, dims[axis]) for axis in range(len(dims))]
    entries = entries.at[tuple(index_at)].set(smallest)
    longest = dims.index(max(dims))
    index_at[longest] = (index_at[longest] + 1) % dims[longest]
    return entries.at[tuple(index_at)].set(largest)


def block_scale(own_key, extent, cuts, smallest, top_value):
    factor_of, own = 1.0, jax.random.fold_in(own_key, 6)
    for dim, shards_of in cuts:
        draws = jnp.exp(jax.random.uniform(jax.random.fold_in(own, dim), (shards_of,), jnp.float32, smallest / len(cuts), top_value / len(cuts)))
        factor_of = factor_of * jnp.repeat(draws, extent[dim] // shards_of).reshape([-1 if axis == dim else 1 for axis in range(len(extent))])
    return factor_of


def centred(own_key, extent, spread, bound, shards=(), held_as=jnp.bfloat16):
    level = block_scale(own_key, extent, shards, -0.22, 0.18) if shards else 1.0
    values = jax.random.normal(own_key, extent, jnp.float32) * spread * level
    return jnp.minimum(jnp.maximum(values, -bound), bound).astype(held_as)


def setup_inputs(seed: int = 0, part: int = 0) -> dict:
    splits = jax.random.split(jax.random.key(seed), 11)
    own_keys = jax.random.split(jax.random.fold_in(splits[10], part), 11)
    return {
        "wave_now": centred(own_keys[0], (2, NY, NZ, NX), 1.0, 6.0, ((1, 16),), jnp.float32),
        "wave_prev": centred(own_keys[1], (2, NY, NZ, NX), 1.0, 6.0, ((1, 16),), jnp.float32),
        "facies": touch_ends(jax.random.randint(splits[2], (NY, NZ, NX), 0, NFAC), jax.random.fold_in(splits[2], 1), 0, NFAC - 1).astype(jnp.int32),
        "velocity_table": jnp.clip(jax.random.uniform(splits[3], (NFAC,), jnp.float32, 0.05, 0.2), 0.05, 0.2),
        "epsilon_table": jnp.clip(jax.random.uniform(splits[4], (NFAC,), jnp.float32, 0.0, 0.2), 0.0, 0.2),
        "tilt_table": jnp.clip(jax.random.uniform(splits[5], (NFAC,), jnp.float32, -0.6, 0.6), -0.6, 0.6),
        "source_cell": jax.random.randint(own_keys[6], (1,), 0, NY * NX).astype(jnp.int32),
        "source_wavelet": centred(own_keys[7], (STEPS,), 2.0, 8.0, (), jnp.float32),
        "receiver_cells": touch_ends(jax.random.randint(own_keys[8], (NREC,), 0, NY * NX), jax.random.fold_in(own_keys[8], 1), 0, (NY * NX) - 1).astype(jnp.int32),
        "receiver_data": centred(own_keys[9], (STEPS, NREC), 1.0, 6.0, (), jnp.float32),
    }


def wave_update(padded, previous, velocity, aniso, tilt):
    center = padded[:, 1:-1, 1:-1, 1:-1]
    along_x = padded[:, 1:-1, 1:-1, 2:] + padded[:, 1:-1, 1:-1, :-2] - 2.0 * center
    along_y = padded[:, 2:, 1:-1, 1:-1] + padded[:, :-2, 1:-1, 1:-1] - 2.0 * center
    along_z = padded[:, 1:-1, 2:, 1:-1] + padded[:, 1:-1, :-2, 1:-1] - 2.0 * center
    mixed = padded[:, 1:-1, 2:, 2:] - padded[:, 1:-1, :-2, 2:] - padded[:, 1:-1, 2:, :-2] + padded[:, 1:-1, :-2, :-2]
    operator = aniso * (along_x + along_y) + along_z + 0.25 * tilt * mixed
    return 2.0 * center - previous + velocity * operator


def filter_planes(extended):
    values = extended.astype(jnp.float32)
    spec = [(0, 0)] * (values.ndim - 3) + [(1, 1), (0, 0), (1, 1)]
    padded = jnp.pad(values, spec)
    center = padded[..., 1:-1, 1:-1, 1:-1]
    neighbours = padded[..., 2:, 1:-1, 1:-1] + padded[..., :-2, 1:-1, 1:-1]
    neighbours = neighbours + padded[..., 1:-1, 2:, 1:-1] + padded[..., 1:-1, :-2, 1:-1]
    neighbours = neighbours + padded[..., 1:-1, 1:-1, 2:] + padded[..., 1:-1, 1:-1, :-2]
    return (0.125 * (6.0 * center - neighbours)).astype(jnp.bfloat16)


def reference(wave_now, wave_prev, facies, velocity_table, epsilon_table, tilt_table, source_cell, source_wavelet, receiver_cells, receiver_data):
    velocity = velocity_table[facies]
    aniso = 1.0 + 2.0 * epsilon_table[facies]
    tilt = tilt_table[facies]
    current, previous = wave_now, wave_prev
    snapshots = []
    for step in range(STEPS):
        padded = jnp.pad(current, ((0, 0), (1, 1), (1, 1), (1, 1)))
        advanced = wave_update(padded, previous, velocity, aniso, tilt)
        source_plane = jnp.zeros((NY * NX,), jnp.float32).at[source_cell].add(jnp.broadcast_to(source_wavelet[step], source_cell.shape))
        receiver_plane = jnp.zeros((NY * NX,), jnp.float32).at[receiver_cells].add(receiver_data[step])
        surface = jnp.stack([source_plane, receiver_plane]).reshape(2, NY, NX)
        advanced = advanced.at[:, :, 0, :].add(surface)
        previous, current = current, advanced
        if step % 2 == 1:
            snapshots.append(current.astype(jnp.bfloat16))
    margin = NLAG // 2
    padded_pairs = []
    for snapshot in snapshots:
        source_padded = jnp.pad(snapshot[0].astype(jnp.float32), ((0, 0), (0, 0), (margin, margin)))
        receiver_padded = jnp.pad(snapshot[1].astype(jnp.float32), ((0, 0), (0, 0), (margin, margin)))
        padded_pairs.append((source_padded, receiver_padded))

    def one_offset(index):
        offset = index - margin
        summed = jnp.zeros((NY, NZ, NX), jnp.float32)
        for source_padded, receiver_padded in padded_pairs:
            left_part = lax.dynamic_slice_in_dim(source_padded, (margin - offset).astype(jnp.int32), NX, 2)
            right_part = lax.dynamic_slice_in_dim(receiver_padded, (margin + offset).astype(jnp.int32), NX, 2)
            summed = summed + left_part * right_part
        image = summed.astype(jnp.bfloat16)
        extended = jnp.pad(image, ((0, 0), (1, 1), (0, 0)))
        return filter_planes(extended[None])[0]

    filtered = lax.map(one_offset, jnp.arange(NLAG, dtype=jnp.int32))
    return filtered, current
```

```python
import functools

import jax
import jax.numpy as jnp
from jax import lax
from jax.experimental import pallas as pl
from jax.experimental.pallas import tpu as pltpu
from jax.sharding import PartitionSpec as P

NLAG = 32
STEPS = 4
REACH = 4
PARTS = 4
LINES = 8


def in_order(count, body):
    def run(i, carry):
        body(i)
        return carry

    lax.fori_loop(0, count, run, 0)


def kernel(
    tiles,
    now,
    prev_in,
    facies_in,
    vel_in,
    eps_in,
    tilt_in,
    src_in,
    wavelet_in,
    cells_in,
    data_in,
    out,
    wave_out,
    own,
    prev,
    facies,
    vel_tab,
    eps_tab,
    tilt_tab,
    src_cell,
    wavelet,
    cells,
    data,
    mate_now,
    mate_prev,
    mate_fac,
    mate_two,
    trace_send,
    trace_recv,
    fac_send,
    fac_recv,
    two,
    work,
    coef,
    far_two,
    lhs,
    surf,
    blocks,
    send,
    recv,
    staged,
    part_image,
    last_own,
    last_sum,
    woven,
    mate_send_sem,
    mate_recv_sem,
    far_send_sem,
    far_recv_sem,
    snap_send,
    snap_recv,
    load_sem,
    near_sem,
):
    rows, depth, cols = facies.shape
    per = depth // tiles
    nrec = data.shape[1]
    group = 2 * rows * (per + 2)
    margin = NLAG // 2
    ngroups = tiles * rows // LINES
    members = LINES // rows
    pairs = (per + 2) // 2
    me = lax.axis_index("tile")
    odd = lax.rem(me, 2)
    even = 1 - odd
    mate = me + 1 - 2 * odd
    far = me - 1 + 2 * odd
    has_far = (far >= 0) & (far < tiles)

    barrier = pltpu.get_barrier_semaphore()

    def signal_at(semaphore, step):
        for way in (-step, step):
            peer = me + way
            there = (peer >= 0) & (peer < tiles)

            @pl.when(there)
            def _():
                pl.semaphore_signal(semaphore, inc=1, device_id={"tile": peer})

    def wait_at(semaphore, step):
        lower = (me >= step).astype(jnp.int32)
        pl.semaphore_wait(semaphore, lower + (me + step < tiles).astype(jnp.int32))

    for step in range(1, min(REACH, tiles - 1) + 1):
        signal_at(barrier, step)

    reaches = []
    while (REACH << len(reaches)) < tiles - 1:
        reaches.append(REACH << len(reaches))

    loads = [
        pltpu.make_async_copy(src, dst, load_sem.at[n])
        for n, (src, dst) in enumerate(
            (
                (cells_in, cells),
                (data_in, data),
                (facies_in, facies),
                (vel_in, vel_tab),
                (eps_in, eps_tab),
                (tilt_in, tilt_tab),
                (src_in, src_cell),
                (wavelet_in, wavelet),
                (now, own),
                (prev_in, prev),
            )
        )
    ]
    for load in loads:
        load.start()
    zero_plane = jnp.zeros((depth, cols), jnp.float32)

    @pl.when(jnp.logical_not(has_far))
    def _():
        for f in range(2):
            for k in range(STEPS):
                trace_recv[k, f] = zero_plane
        for n in range(2):
            fac_recv[n] = jnp.full((depth, cols), -1.0, jnp.bfloat16)

    def remote(src, dst, ssem, rsem, peer):
        return pltpu.make_async_remote_copy(
            src_ref=src, dst_ref=dst, send_sem=ssem, recv_sem=rsem, device_id={"tile": peer}
        )

    def mate_copy(n, src, dst):
        return remote(src, dst, mate_send_sem.at[n], mate_recv_sem.at[n], mate)

    def far_copy(n, src, dst):
        return remote(src, dst, far_send_sem.at[n], far_recv_sem.at[n], far)

    mate_first = (
        mate_copy(0, own, mate_now),
        mate_copy(1, prev.at[:, even], mate_prev),
        mate_copy(2, facies.at[even], mate_fac),
    )
    mate_second = mate_copy(3, two, mate_two)
    far_first = (
        far_copy(0, fac_send, fac_recv),
        far_copy(1, own.at[:, odd], trace_recv.at[0]),
        far_copy(2, trace_send.at[0], trace_recv.at[1]),
    )
    far_second = far_copy(3, trace_send.at[1:3], trace_recv.at[2:4])

    lines = (me * rows + odd, me * rows + even, mate * rows + odd)

    for load in loads[:2]:
        load.wait()

    cell = cells[...]
    column = cell & (cols - 1) if cols & (cols - 1) == 0 else lax.rem(cell, cols)
    onehot = (lax.broadcasted_iota(jnp.int32, (cols, nrec), 0) == column).astype(jnp.float32)
    onehot = onehot.astype(jnp.bfloat16)
    amounts = data[...]
    high = amounts.astype(jnp.bfloat16).astype(jnp.float32)
    rest = amounts - high
    middle = rest.astype(jnp.bfloat16).astype(jnp.float32)
    parts = (high, middle, rest - middle, jnp.zeros_like(high))
    for i in range(3):
        first = lines[i] * cols
        inside = (cell >= first) & (cell < first + cols)
        for p, part in enumerate(parts):
            at = (i * PARTS + p) * STEPS
            lhs[at : at + STEPS, :] = jnp.where(inside, part, 0.0)
    surf[...] = lax.dot_general(
        lhs[...].astype(jnp.bfloat16), onehot, (((1,), (1,)), ((), ())),
        preferred_element_type=jnp.float32,
    )

    def looked_up(kinds):
        vel = jnp.zeros((depth, cols), jnp.float32)
        eps, tlt = vel, vel
        for n in range(vel_tab.shape[0]):
            here = kinds == n
            vel = jnp.where(here, vel_tab[n], vel)
            eps = jnp.where(here, eps_tab[n], eps)
            tlt = jnp.where(here, tilt_tab[n], tlt)
        return vel, vel * (1.0 + 2.0 * eps), 0.25 * vel * tlt

    def fill_coef(i, kinds):
        vel, flat, tlt = looked_up(kinds)
        coef[0, i] = 2.0 - 4.0 * flat - 2.0 * vel
        coef[1, i] = flat
        coef[2, i] = vel
        coef[3, i] = tlt

    lane = lax.broadcasted_iota(jnp.int32, (depth, cols), 1)
    level = lax.broadcasted_iota(jnp.int32, (depth, cols), 0)
    first_lane, last_lane = lane == 0, lane == cols - 1
    first_level, last_level = level == 0, level == depth - 1
    surface_lane = lax.broadcasted_iota(jnp.int32, (1, cols), 1)

    def advance(i, current, above, below, old):
        right = lambda v: jnp.where(last_lane, 0.0, pltpu.roll(v, cols - 1, 1))
        left = lambda v: jnp.where(first_lane, 0.0, pltpu.roll(v, 1, 1))
        deeper = jnp.where(last_level, 0.0, pltpu.roll(current, depth - 1, 0))
        higher = jnp.where(first_level, 0.0, pltpu.roll(current, 1, 0))
        slope = deeper - higher
        flat = right(current) + left(current)
        if above is not None:
            flat = flat + above
        if below is not None:
            flat = flat + below
        mixed = right(slope) - left(slope)
        new = coef[0, i] * current + coef[1, i] * flat + coef[2, i] * (deeper + higher)
        new = new + coef[3, i] * mixed
        return new if old is None else new - old

    def inject(step, f, i, new):
        if f == 0:
            added = jnp.where(surface_lane == src_cell[0] - lines[i] * cols, wavelet[step], 0.0)
        else:
            at = i * PARTS * STEPS + step
            added = surf[at : at + 1, :]
            for p in range(1, 3):
                added = added + surf[at + p * STEPS : at + p * STEPS + 1, :]
        return new + jnp.where(first_level, added, 0.0)

    for load in loads[2:]:
        load.wait()
    fac_send[0] = facies[odd].astype(jnp.float32).astype(jnp.bfloat16)
    fac_send[1] = facies[even].astype(jnp.float32).astype(jnp.bfloat16)
    fill_coef(0, facies[odd])
    for f in range(2):
        new = advance(0, own[f, odd], None, own[f, even], prev[f, odd])
        trace_send[0, f] = inject(0, f, 0, new)
    fill_coef(1, facies[even])

    reach = min(REACH, tiles - 1)
    pl.semaphore_wait(barrier, jnp.minimum(me, reach) + jnp.minimum(tiles - 1 - me, reach))

    for copy in mate_first:
        copy.start()

    @pl.when(has_far)
    def _():
        for copy in far_first:
            copy.start()

    if reaches:
        signal_at(near_sem.at[0], reaches[0])

    blocks[group : 2 * group, :] = jnp.zeros((group, cols), jnp.float32)
    blocks[group * tiles : group * (tiles + 1), :] = jnp.zeros((group, cols), jnp.float32)
    zero_lines = jnp.zeros((per, LINES, cols), jnp.float32)
    for k in range(NLAG):
        last_own[k] = zero_lines
        last_sum[k] = zero_lines

    for copy in mate_first:
        copy.wait_recv()
    fill_coef(2, mate_fac[...])
    for f in range(2):
        work[0, f] = inject(
            0, f, 1, advance(1, own[f, even], own[f, odd], mate_now[f, odd], prev[f, even])
        )
        work[1, f] = inject(
            0, f, 2, advance(2, mate_now[f, odd], own[f, even], mate_now[f, even], mate_prev[f])
        )
    for f in range(2):
        one = trace_send[0, f]
        new = inject(1, f, 0, advance(0, one, None, work[0, f], own[f, odd]))
        trace_send[1, f] = new
        near = inject(1, f, 1, advance(1, work[0, f], one, work[1, f], own[f, even]))
        work[2, f] = near
        trace_send[2, f] = inject(2, f, 0, advance(0, new, None, near, one))

    @pl.when(has_far)
    def _():
        far_second.start()

    if reaches:
        wait_at(near_sem.at[0], reaches[0])
    if len(reaches) > 1:
        signal_at(near_sem.at[1], reaches[1])

    @pl.when(has_far)
    def _():
        for copy in far_first:
            copy.wait_recv()

    fill_coef(3, fac_recv[0].astype(jnp.float32))
    for f in range(2):
        push = coef[1, 0] * trace_recv[0, f]
        one = trace_send[0, f] + push
        echo = coef[1, 3] * own[f, odd]
        new = advance(0, one, trace_recv[1, f] + echo, work[0, f], own[f, odd])
        two[f, odd] = inject(1, f, 0, new)
        two[f, even] = work[2, f] + coef[1, 1] * push
        work[3, f] = one
        work[4, f] = echo
    mate_second.start()

    def pack_snapshot(s, source):
        for r in range(rows):
            for f in range(2):
                at = (r * 2 + f) * (per + 2)
                upper = source[f, r, pl.ds(0, tiles, stride=2), :]
                lower = source[f, r, pl.ds(1, tiles, stride=2), :]
                blocks[pl.ds(at + 2 * group, tiles, stride=group), :] = lower
                blocks[pl.ds(at + group + 1, tiles, stride=group), :] = upper
                blocks[pl.ds(at + group + 2, tiles, stride=group), :] = lower
                blocks[pl.ds(at + 3, tiles, stride=group), :] = upper
        for d in range(tiles):
            at = (d + 1) * group
            send[s, d] = blocks[at : at + group, :].astype(jnp.bfloat16)

    def snap_copy(s, peer):
        return remote(
            send.at[s, peer], recv.at[s, me], snap_send.at[s, peer], snap_recv.at[s, me], peer
        )

    def each_peer(action):
        def body(peer):
            @pl.when(peer != me)
            def _():
                action(peer)

        in_order(tiles, body)

    def send_snapshot(s):
        each_peer(lambda peer: snap_copy(s, peer).start())
        recv[s, me] = send[s, me]

    pack_snapshot(0, two)
    for n in range(1, len(reaches)):
        wait_at(near_sem.at[n], reaches[n])
        if n + 1 < len(reaches):
            signal_at(near_sem.at[n + 1], reaches[n + 1])
    send_snapshot(0)

    far_two[...] = looked_up(fac_recv[1].astype(jnp.float32))[1]
    for f in range(2):
        work[5, f] = advance(3, work[4, f], work[3, f], None, None)

    @pl.when(has_far)
    def _():
        far_second.wait_recv()

    for f in range(2):
        echo, echo_two = work[4, f], work[5, f]
        new = advance(0, two[f, odd], trace_recv[2, f] + echo_two, two[f, even], work[3, f])
        work[6, f] = inject(2, f, 0, new)
        behind = far_two[...] * echo
        work[7, f] = trace_recv[3, f] + advance(3, echo_two, two[f, odd], behind, echo)

    mate_second.wait_recv()
    for f in range(2):
        near = inject(
            2, f, 1, advance(1, two[f, even], two[f, odd], mate_two[f, odd], work[0, f])
        )
        beyond = inject(
            2, f, 2, advance(2, mate_two[f, odd], two[f, even], mate_two[f, even], work[1, f])
        )
        edge = work[6, f]
        wave_out[f, odd] = inject(3, f, 0, advance(0, edge, work[7, f], near, two[f, odd]))
        wave_out[f, even] = inject(3, f, 1, advance(1, near, edge, beyond, two[f, even]))
    pack_snapshot(1, wave_out)
    send_snapshot(1)

    image_lane = lax.broadcasted_iota(jnp.int32, (1, cols), 1)
    line = lax.broadcasted_iota(jnp.int32, (LINES, cols), 0)
    last_line = line == LINES - 1

    def arrived(s, g):
        for i in range(members):
            peer = g * members + i

            @pl.when(peer != me)
            def _():
                remote(
                    send.at[s, me], recv.at[s, peer], snap_send.at[s, me], snap_recv.at[s, peer], peer
                ).wait_recv()

        for i in range(members):
            staged[s, i * group : (i + 1) * group, :] = recv[s, g * members + i].astype(jnp.float32)
        lifted = lambda f, j: staged[
            s, pl.ds(f * (per + 2) + j, LINES, stride=2 * (per + 2)), :
        ]
        return [
            [
                jnp.concatenate([lifted(f, j), lifted(f, j + 1)], axis=0)
                for j in range(0, per + 2, 2)
            ]
            for f in range(2)
        ]

    def turned(values, amount):
        amount = amount % cols
        return pltpu.roll(values, amount, 1) if amount else values

    def first_products(g):
        ahead, behind = arrived(0, g)
        behind = [v.astype(jnp.bfloat16) for v in behind]
        for k in range(NLAG):
            for j in range(pairs):
                pulled = turned(behind[j], 2 * (margin - k)).astype(jnp.float32)
                part_image[g, k, j] = ahead[j] * pulled

    def finish(g, last):
        ahead, behind = arrived(1, g)
        behind = [v.astype(jnp.bfloat16) for v in behind]

        def write(slot, h, at, results):
            for z in range(per):
                woven[slot, pl.ds(z, LINES, stride=per), :] = results[z]
            out[h + margin, at] = turned(woven[slot].astype(jnp.bfloat16), h)

        for k in range(NLAG):
            h = k - margin
            products = [
                part_image[g, k, j] + ahead[j] * turned(behind[j], -2 * h).astype(jnp.float32)
                for j in range(pairs)
            ]
            if h > 0:
                products = [jnp.where(image_lane < cols - 2 * h, v, 0.0) for v in products]
            elif h < 0:
                products = [jnp.where(image_lane >= -2 * h, v, 0.0) for v in products]
            image = jnp.concatenate(products, axis=0)
            image = image.astype(jnp.bfloat16).astype(jnp.float32)
            plane = [image[j * LINES : (j + 1) * LINES] for j in range(per + 2)]
            before, sums = [], []
            for z in range(per):
                mine = plane[z + 1]
                lower, higher = turned(mine, 1), turned(mine, -1)
                if h == 0:
                    lower = jnp.where(image_lane == 0, 0.0, lower)
                    higher = jnp.where(image_lane == cols - 1, 0.0, higher)
                total = (lower + higher) + (plane[z] + plane[z + 2])
                total = total + pltpu.roll(jnp.where(last_line, last_own[k, z], mine), 1, 0)
                later = pltpu.roll(mine, LINES - 1, 0)
                total = total + jnp.where(last_line, 0.0, later)
                before.append(0.125 * (last_sum[k, z] - jnp.where(last_line, later, 0.0)))
                sums.append(6.0 * mine - total)
            if last:
                if ngroups > 1:
                    write(2 * k, h, g - 1, before)
                write(2 * k + 1, h, g, [0.125 * value for value in sums])
            else:
                write(2 * k, h, jnp.maximum(g - 1, 0), before)
                for z in range(per):
                    last_own[k, z] = plane[z + 1]
                    last_sum[k, z] = sums[z]

    first_products(0)

    def both(g):
        first_products(g + 1)
        finish(g, False)

    in_order(ngroups - 1, both)
    finish(ngroups - 1, True)

    for copy in mate_first:
        copy.wait_send()
    mate_second.wait_send()

    @pl.when(has_far)
    def _():
        for copy in far_first:
            copy.wait_send()
        far_second.wait_send()

    for s in range(2):
        each_peer(lambda peer: snap_copy(s, peer).wait_send())


def shards(tiles, now, prev, facies, vel, eps, tilt, src_cell, wavelet, cells, data):
    rows, depth, cols = facies.shape
    per = depth // tiles
    nrec = cells.shape[0]
    group = 2 * rows * (per + 2)
    ngroups = tiles * rows // LINES
    assert rows == 2 and per == 2 and tiles * rows % LINES == 0
    f32 = jnp.float32
    vmem = pl.BlockSpec(memory_space=pltpu.VMEM)
    hbm = pl.BlockSpec(memory_space=pltpu.HBM)
    lhs_rows = 3 * PARTS * STEPS
    plane = (depth, cols)
    filtered, wave = pl.pallas_call(
        functools.partial(kernel, tiles),
        out_shape=(
            pltpu.VMEM((NLAG, ngroups, LINES * per, cols), jnp.bfloat16),
            pltpu.VMEM(now.shape, f32),
        ),
        in_specs=[hbm] * 10,
        out_specs=(vmem, vmem),
        scratch_shapes=[
            pltpu.VMEM(now.shape, f32),
            pltpu.VMEM(prev.shape, f32),
            pltpu.VMEM(facies.shape, jnp.int32),
            pltpu.SMEM(vel.shape, f32),
            pltpu.SMEM(eps.shape, f32),
            pltpu.SMEM(tilt.shape, f32),
            pltpu.SMEM(src_cell.shape, jnp.int32),
            pltpu.SMEM(wavelet.shape, f32),
            pltpu.VMEM((1, nrec), jnp.int32),
            pltpu.VMEM(data.shape, f32),
            pltpu.VMEM(now.shape, f32),
            pltpu.VMEM((2, *plane), f32),
            pltpu.VMEM(plane, jnp.int32),
            pltpu.VMEM(now.shape, f32),
            pltpu.VMEM((3, 2, *plane), f32),
            pltpu.VMEM((4, 2, *plane), f32),
            pltpu.VMEM((2, *plane), jnp.bfloat16),
            pltpu.VMEM((2, *plane), jnp.bfloat16),
            pltpu.VMEM(now.shape, f32),
            pltpu.VMEM((8, 2, *plane), f32),
            pltpu.VMEM((4, 4, *plane), f32),
            pltpu.VMEM(plane, f32),
            pltpu.VMEM((lhs_rows, nrec), f32),
            pltpu.VMEM((lhs_rows, cols), f32),
            pltpu.VMEM(((tiles + 2) * group, cols), f32),
            pltpu.VMEM((2, tiles, group, cols), jnp.bfloat16),
            pltpu.VMEM((2, tiles, group, cols), jnp.bfloat16),
            pltpu.VMEM((2, LINES // rows * group, cols), f32),
            pltpu.VMEM((ngroups, NLAG, (per + 2) // 2, 2 * LINES, cols), f32),
            pltpu.VMEM((NLAG, per, LINES, cols), f32),
            pltpu.VMEM((NLAG, per, LINES, cols), f32),
            pltpu.VMEM((2 * NLAG, LINES * per, cols), f32),
            pltpu.SemaphoreType.DMA((4,)),
            pltpu.SemaphoreType.DMA((4,)),
            pltpu.SemaphoreType.DMA((4,)),
            pltpu.SemaphoreType.DMA((4,)),
            pltpu.SemaphoreType.DMA((2, tiles)),
            pltpu.SemaphoreType.DMA((2, tiles)),
            pltpu.SemaphoreType.DMA((10,)),
            pltpu.SemaphoreType.REGULAR((max(1, tiles.bit_length()),)),
        ],
        compiler_params=pltpu.CompilerParams(collective_id=0, has_side_effects=True),
    )(now, prev, facies, vel, eps, tilt, src_cell, wavelet, cells.reshape(1, nrec), data)
    return filtered.reshape(NLAG, rows * tiles, per, cols), wave


def solution(mesh):
    return jax.shard_map(
        functools.partial(shards, mesh.shape["tile"]),
        mesh=mesh,
        in_specs=(
            P("shot", "tile", None, None),
            P("shot", "tile", None, None),
            P("tile", None, None),
            P(),
            P(),
            P(),
            P("shot"),
            P("shot"),
            P("shot"),
            P(None, "shot"),
        ),
        out_specs=(P("shot", None, "tile", None), P("shot", "tile", None, None)),
        check_vma=False,
    )
```

```python
import functools

import jax
import jax.numpy as jnp
from jax import lax
from jax.experimental import pallas as pl
from jax.experimental.pallas import tpu as pltpu
from jax.sharding import PartitionSpec as P

NLAG = 32
STEPS = 4
REACH = 4
PARTS = 4
LINES = 8


def in_order(count, body):
    def run(i, carry):
        body(i)
        return carry

    lax.fori_loop(0, count, run, 0)


def kernel(
    tiles,
    now,
    prev_in,
    facies_in,
    vel_in,
    eps_in,
    tilt_in,
    src_in,
    wavelet_in,
    cells_in,
    data_in,
    out,
    wave_out,
    own,
    prev,
    facies,
    vel_tab,
    eps_tab,
    tilt_tab,
    src_cell,
    wavelet,
    cells,
    data,
    mate_now,
    mate_prev,
    mate_fac,
    mate_two,
    trace_send,
    trace_recv,
    fac_send,
    fac_recv,
    two,
    work,
    coef,
    far_two,
    lhs,
    surf,
    blocks,
    send,
    recv,
    staged,
    part_image,
    last_own,
    last_sum,
    woven,
    mate_send_sem,
    mate_recv_sem,
    far_send_sem,
    far_recv_sem,
    snap_send,
    snap_recv,
    load_sem,
    near_sem,
):
    rows, depth, cols = facies.shape
    per = depth // tiles
    nrec = data.shape[1]
    group = 2 * rows * (per + 2)
    margin = NLAG // 2
    ngroups = tiles * rows // LINES
    members = LINES // rows
    pairs = (per + 2) // 2
    me = lax.axis_index("tile")
    odd = lax.rem(me, 2)
    even = 1 - odd
    mate = me + 1 - 2 * odd
    far = me - 1 + 2 * odd
    has_far = (far >= 0) & (far < tiles)

    loads = [
        pltpu.make_async_copy(src, dst, load_sem.at[n])
        for n, (src, dst) in enumerate(
            (
                (now, own),
                (prev_in, prev),
                (facies_in, facies),
                (vel_in, vel_tab),
                (eps_in, eps_tab),
                (tilt_in, tilt_tab),
                (cells_in, cells),
                (data_in, data),
                (src_in, src_cell),
                (wavelet_in, wavelet),
            )
        )
    ]
    for load in loads:
        load.start()
    barrier = pltpu.get_barrier_semaphore()

    def signal_at(semaphore, step):
        for way in (-step, step):
            peer = me + way
            there = (peer >= 0) & (peer < tiles)

            @pl.when(there)
            def _():
                pl.semaphore_signal(semaphore, inc=1, device_id={"tile": peer})

    def wait_at(semaphore, step):
        lower = (me >= step).astype(jnp.int32)
        pl.semaphore_wait(semaphore, lower + (me + step < tiles).astype(jnp.int32))

    for step in range(1, min(REACH, tiles - 1) + 1):
        signal_at(barrier, step)

    reaches = []
    while (REACH << len(reaches)) < tiles - 1:
        reaches.append(REACH << len(reaches))

    zero_plane = jnp.zeros((depth, cols), jnp.float32)

    @pl.when(jnp.logical_not(has_far))
    def _():
        for f in range(2):
            for k in range(STEPS):
                trace_recv[k, f] = zero_plane
        for n in range(2):
            fac_recv[n] = jnp.full((depth, cols), -1.0, jnp.bfloat16)

    def remote(src, dst, ssem, rsem, peer):
        return pltpu.make_async_remote_copy(
            src_ref=src, dst_ref=dst, send_sem=ssem, recv_sem=rsem, device_id={"tile": peer}
        )

    def mate_copy(n, src, dst):
        return remote(src, dst, mate_send_sem.at[n], mate_recv_sem.at[n], mate)

    def far_copy(n, src, dst):
        return remote(src, dst, far_send_sem.at[n], far_recv_sem.at[n], far)

    mate_first = (
        mate_copy(0, own, mate_now),
        mate_copy(1, prev.at[:, even], mate_prev),
        mate_copy(2, facies.at[even], mate_fac),
    )
    mate_second = mate_copy(3, two, mate_two)
    far_fac = far_copy(0, fac_send.at[0], fac_recv.at[0])
    far_deep = far_copy(1, fac_send.at[1], fac_recv.at[1])
    far_now = far_copy(2, own.at[:, odd], trace_recv.at[0])
    far_one, far_second, far_third = (
        far_copy(3 + k, trace_send.at[k], trace_recv.at[k + 1]) for k in range(3)
    )
    far_all = (far_fac, far_now, far_one, far_deep, far_second, far_third)

    def from_far(*copies):
        @pl.when(has_far)
        def _():
            for copy in copies:
                copy.wait_recv()

    def to_far(*copies):
        @pl.when(has_far)
        def _():
            for copy in copies:
                copy.start()

    lines = (me * rows + odd, me * rows + even, mate * rows + odd, far * rows + even)

    def looked_up(kinds):
        vel = jnp.zeros((depth, cols), jnp.float32)
        eps, tlt = vel, vel
        for n in range(vel_tab.shape[0]):
            here = kinds == n
            vel = jnp.where(here, vel_tab[n], vel)
            eps = jnp.where(here, eps_tab[n], eps)
            tlt = jnp.where(here, tilt_tab[n], tlt)
        return vel, vel * (1.0 + 2.0 * eps), 0.25 * vel * tlt

    lane = lax.broadcasted_iota(jnp.int32, (depth, cols), 1)
    level = lax.broadcasted_iota(jnp.int32, (depth, cols), 0)
    first_lane, last_lane = lane == 0, lane == cols - 1
    first_level, last_level = level == 0, level == depth - 1
    surface_lane = lax.broadcasted_iota(jnp.int32, (1, cols), 1)

    to_right = lambda v: pltpu.roll(v, 1, 1)
    to_left = lambda v: pltpu.roll(v, cols - 1, 1)

    def fill_coef(i, kinds):
        vel, flat, tlt = looked_up(kinds)
        coef[0, i] = 2.0 - 4.0 * flat - 2.0 * vel
        coef[1, i] = flat
        coef[2, i] = vel
        coef[3, i] = jnp.where(first_lane, 0.0, to_right(flat))
        coef[4, i] = jnp.where(first_lane, 0.0, to_right(tlt))
        coef[5, i] = jnp.where(last_lane, 0.0, to_left(flat))
        coef[6, i] = jnp.where(last_lane, 0.0, to_left(tlt))

    def advance(i, current, above, below, old):
        deeper = jnp.where(last_level, 0.0, pltpu.roll(current, depth - 1, 0))
        higher = jnp.where(first_level, 0.0, pltpu.roll(current, 1, 0))
        slope = deeper - higher
        new = to_left(coef[3, i] * current + coef[4, i] * slope)
        new = new + to_right(coef[5, i] * current - coef[6, i] * slope)
        new = new + coef[2, i] * (deeper + higher) + coef[0, i] * current
        if above is not None:
            new = new + coef[1, i] * (above if below is None else above + below)
        elif below is not None:
            new = new + coef[1, i] * below
        return new if old is None else new - old

    def inject(step, f, i, new):
        if f == 0:
            added = jnp.where(surface_lane == src_cell[0] - lines[i] * cols, wavelet[step], 0.0)
        else:
            at = i * PARTS * STEPS + step
            added = surf[at : at + 1, :]
            for p in range(1, 3):
                added = added + surf[at + p * STEPS : at + p * STEPS + 1, :]
        return new + jnp.where(first_level, added, 0.0)

    for load in loads[:6]:
        load.wait()
    fac_send[0] = facies[odd].astype(jnp.float32).astype(jnp.bfloat16)
    fac_send[1] = facies[even].astype(jnp.float32).astype(jnp.bfloat16)
    fill_coef(0, facies[odd])
    for f in range(2):
        trace_send[0, f] = advance(0, own[f, odd], None, own[f, even], prev[f, odd])
    reach = min(REACH, tiles - 1)
    pl.semaphore_wait(barrier, jnp.minimum(me, reach) + jnp.minimum(tiles - 1 - me, reach))

    to_far(far_fac, far_now, far_one)
    for copy in mate_first:
        copy.start()
    to_far(far_deep)

    if reaches:
        signal_at(near_sem.at[0], reaches[0])

    for load in loads[6:]:
        load.wait()

    cell = cells[...]
    column = cell & (cols - 1) if cols & (cols - 1) == 0 else lax.rem(cell, cols)
    onehot = (lax.broadcasted_iota(jnp.int32, (cols, nrec), 0) == column).astype(jnp.float32)
    onehot = onehot.astype(jnp.bfloat16)
    amounts = data[...]
    high = amounts.astype(jnp.bfloat16).astype(jnp.float32)
    rest = amounts - high
    middle = rest.astype(jnp.bfloat16).astype(jnp.float32)
    parts = (high, middle, rest - middle, jnp.zeros_like(high))
    for i in range(4):
        first = lines[i] * cols
        inside = (cell >= first) & (cell < first + cols)
        for p, part in enumerate(parts):
            at = (i * PARTS + p) * STEPS
            lhs[at : at + STEPS, :] = jnp.where(inside, part, 0.0)
    surf[...] = lax.dot_general(
        lhs[...].astype(jnp.bfloat16), onehot, (((1,), (1,)), ((), ())),
        preferred_element_type=jnp.float32,
    )

    for f in range(2):
        work[3, f] = inject(0, f, 0, trace_send[0, f])
    fill_coef(1, facies[even])
    blocks[group : 2 * group, :] = jnp.zeros((group, cols), jnp.float32)
    blocks[group * tiles : group * (tiles + 1), :] = jnp.zeros((group, cols), jnp.float32)
    zero_lines = jnp.zeros((per, LINES, cols), jnp.float32)
    for k in range(NLAG):
        last_own[k] = zero_lines
        last_sum[k] = zero_lines

    mate_first[0].wait_recv()
    for f in range(2):
        work[0, f] = inject(
            0, f, 1, advance(1, own[f, even], own[f, odd], mate_now[f, odd], prev[f, even])
        )
        trace_send[1, f] = inject(
            1, f, 0, advance(0, work[3, f], None, work[0, f], own[f, odd])
        )
    to_far(far_second)
    for copy in mate_first[1:]:
        copy.wait_recv()
    fill_coef(2, mate_fac[...])
    for f in range(2):
        work[1, f] = inject(
            0, f, 2, advance(2, mate_now[f, odd], own[f, even], mate_now[f, even], mate_prev[f])
        )
        near = inject(1, f, 1, advance(1, work[0, f], work[3, f], work[1, f], own[f, even]))
        work[2, f] = near
        trace_send[2, f] = inject(2, f, 0, advance(0, trace_send[1, f], None, near, work[3, f]))
    to_far(far_third)

    if reaches:
        wait_at(near_sem.at[0], reaches[0])
    if len(reaches) > 1:
        signal_at(near_sem.at[1], reaches[1])

    from_far(far_fac, far_now, far_one)

    fill_coef(3, fac_recv[0].astype(jnp.float32))
    for f in range(2):
        push = coef[1, 0] * trace_recv[0, f]
        one = work[3, f] + push
        echo = coef[1, 3] * own[f, odd]
        beside = inject(0, f, 3, trace_recv[1, f]) + echo
        new = advance(0, one, beside, work[0, f], own[f, odd])
        two[f, odd] = inject(1, f, 0, new)
        two[f, even] = work[2, f] + coef[1, 1] * push
        work[3, f] = one
        work[4, f] = echo
    mate_second.start()

    def pack_snapshot(s, source):
        for r in range(rows):
            for f in range(2):
                at = (r * 2 + f) * (per + 2)
                upper = source[f, r, pl.ds(0, tiles, stride=2), :]
                lower = source[f, r, pl.ds(1, tiles, stride=2), :]
                blocks[pl.ds(at + 2 * group, tiles, stride=group), :] = lower
                blocks[pl.ds(at + group + 1, tiles, stride=group), :] = upper
                blocks[pl.ds(at + group + 2, tiles, stride=group), :] = lower
                blocks[pl.ds(at + 3, tiles, stride=group), :] = upper
        for d in range(tiles):
            at = (d + 1) * group
            send[s, d] = blocks[at : at + group, :].astype(jnp.bfloat16)

    def snap_copy(s, peer):
        return remote(
            send.at[s, peer], recv.at[s, me], snap_send.at[s, peer], snap_recv.at[s, me], peer
        )

    def each_peer(action):
        def body(peer):
            @pl.when(peer != me)
            def _():
                action(peer)

        in_order(tiles, body)

    def send_snapshot(s):
        each_peer(lambda peer: snap_copy(s, peer).start())
        recv[s, me] = send[s, me]

    pack_snapshot(0, two)
    for n in range(1, len(reaches)):
        wait_at(near_sem.at[n], reaches[n])
        if n + 1 < len(reaches):
            signal_at(near_sem.at[n + 1], reaches[n + 1])
    send_snapshot(0)

    from_far(far_deep)
    far_two[...] = looked_up(fac_recv[1].astype(jnp.float32))[1]
    for f in range(2):
        echo = work[4, f]
        echo_two = advance(3, echo, work[3, f], None, None)
        work[5, f] = advance(3, echo_two, two[f, odd], far_two[...] * echo, echo)
        new = advance(0, two[f, odd], echo_two, two[f, even], work[3, f])
        work[6, f] = inject(2, f, 0, new)
        new = advance(1, two[f, even], two[f, odd], None, work[0, f])
        work[7, f] = inject(2, f, 1, new)

    from_far(far_second)
    for f in range(2):
        work[6, f] = work[6, f] + coef[1, 0] * trace_recv[2, f]
    mate_second.wait_recv()
    for f in range(2):
        edge = work[6, f]
        near = work[7, f] + coef[1, 1] * mate_two[f, odd]
        beyond = inject(
            2, f, 2, advance(2, mate_two[f, odd], two[f, even], mate_two[f, even], work[1, f])
        )
        wave_out[f, odd] = inject(3, f, 0, advance(0, edge, work[5, f], near, two[f, odd]))
        wave_out[f, even] = inject(3, f, 1, advance(1, near, edge, beyond, two[f, even]))
    from_far(far_third)
    for f in range(2):
        wave_out[f, odd] = wave_out[f, odd] + coef[1, 0] * trace_recv[3, f]
    pack_snapshot(1, wave_out)
    send_snapshot(1)

    image_lane = lax.broadcasted_iota(jnp.int32, (1, cols), 1)
    line = lax.broadcasted_iota(jnp.int32, (LINES, cols), 0)
    last_line = line == LINES - 1

    def arrived(s, g):
        for i in range(members):
            peer = g * members + i

            @pl.when(peer != me)
            def _():
                remote(
                    send.at[s, me], recv.at[s, peer], snap_send.at[s, me], snap_recv.at[s, peer], peer
                ).wait_recv()

        for i in range(members):
            staged[s, i * group : (i + 1) * group, :] = recv[s, g * members + i].astype(jnp.float32)
        lifted = lambda f, j: staged[
            s, pl.ds(f * (per + 2) + j, LINES, stride=2 * (per + 2)), :
        ]
        return [
            [
                jnp.concatenate([lifted(f, j), lifted(f, j + 1)], axis=0)
                for j in range(0, per + 2, 2)
            ]
            for f in range(2)
        ]

    def turned(values, amount):
        amount = amount % cols
        return pltpu.roll(values, amount, 1) if amount else values

    def first_products(g):
        ahead, behind = arrived(0, g)
        behind = [v.astype(jnp.bfloat16) for v in behind]
        for k in range(NLAG):
            for j in range(pairs):
                pulled = turned(behind[j], 2 * (margin - k)).astype(jnp.float32)
                part_image[g, k, j] = ahead[j] * pulled

    def finish(g, last):
        ahead, behind = arrived(1, g)
        behind = [v.astype(jnp.bfloat16) for v in behind]

        def write(slot, h, at, results):
            for z in range(per):
                woven[slot, pl.ds(z, LINES, stride=per), :] = results[z]
            out[h + margin, at] = turned(woven[slot].astype(jnp.bfloat16), h)

        for k in range(NLAG):
            h = k - margin
            products = [
                part_image[g, k, j] + ahead[j] * turned(behind[j], -2 * h).astype(jnp.float32)
                for j in range(pairs)
            ]
            if h > 0:
                products = [jnp.where(image_lane < cols - 2 * h, v, 0.0) for v in products]
            elif h < 0:
                products = [jnp.where(image_lane >= -2 * h, v, 0.0) for v in products]
            image = jnp.concatenate(products, axis=0)
            image = image.astype(jnp.bfloat16).astype(jnp.float32)
            plane = [image[j * LINES : (j + 1) * LINES] for j in range(per + 2)]
            before, sums = [], []
            for z in range(per):
                mine = plane[z + 1]
                lower, higher = turned(mine, 1), turned(mine, -1)
                if h == 0:
                    lower = jnp.where(image_lane == 0, 0.0, lower)
                    higher = jnp.where(image_lane == cols - 1, 0.0, higher)
                total = (lower + higher) + (plane[z] + plane[z + 2])
                total = total + pltpu.roll(jnp.where(last_line, last_own[k, z], mine), 1, 0)
                later = pltpu.roll(mine, LINES - 1, 0)
                total = total + jnp.where(last_line, 0.0, later)
                before.append(0.125 * (last_sum[k, z] - jnp.where(last_line, later, 0.0)))
                sums.append(6.0 * mine - total)
            if last:
                if ngroups > 1:
                    write(2 * k, h, g - 1, before)
                write(2 * k + 1, h, g, [0.125 * value for value in sums])
            else:
                write(2 * k, h, jnp.maximum(g - 1, 0), before)
                for z in range(per):
                    last_own[k, z] = plane[z + 1]
                    last_sum[k, z] = sums[z]

    first_products(0)

    def both(g):
        first_products(g + 1)
        finish(g, False)

    in_order(ngroups - 1, both)
    for copy in mate_first:
        copy.wait_send()
    mate_second.wait_send()

    @pl.when(has_far)
    def _():
        for copy in far_all:
            copy.wait_send()

    for s in range(2):
        each_peer(lambda peer: snap_copy(s, peer).wait_send())

    finish(ngroups - 1, True)

def stored(filtered_in, wave_in, filtered, wave, sems):
    copies = [
        pltpu.make_async_copy(src, dst, sems.at[n])
        for n, (src, dst) in enumerate(((filtered_in, filtered), (wave_in, wave)))
    ]
    for copy in copies:
        copy.start()
    for copy in copies:
        copy.wait()


def shards(tiles, now, prev, facies, vel, eps, tilt, src_cell, wavelet, cells, data):
    rows, depth, cols = facies.shape
    per = depth // tiles
    nrec = cells.shape[0]
    group = 2 * rows * (per + 2)
    ngroups = tiles * rows // LINES
    assert rows == 2 and per == 2 and tiles * rows % LINES == 0
    f32 = jnp.float32
    vmem = pl.BlockSpec(memory_space=pltpu.VMEM)
    hbm = pl.BlockSpec(memory_space=pltpu.HBM)
    lhs_rows = 4 * PARTS * STEPS
    plane = (depth, cols)
    filtered, wave = pl.pallas_call(
        functools.partial(kernel, tiles),
        out_shape=(
            pltpu.VMEM((NLAG, ngroups, LINES * per, cols), jnp.bfloat16),
            pltpu.VMEM(now.shape, f32),
        ),
        in_specs=[hbm] * 10,
        out_specs=(vmem, vmem),
        scratch_shapes=[
            pltpu.VMEM(now.shape, f32),
            pltpu.VMEM(prev.shape, f32),
            pltpu.VMEM(facies.shape, jnp.int32),
            pltpu.SMEM(vel.shape, f32),
            pltpu.SMEM(eps.shape, f32),
            pltpu.SMEM(tilt.shape, f32),
            pltpu.SMEM(src_cell.shape, jnp.int32),
            pltpu.SMEM(wavelet.shape, f32),
            pltpu.VMEM((1, nrec), jnp.int32),
            pltpu.VMEM(data.shape, f32),
            pltpu.VMEM(now.shape, f32),
            pltpu.VMEM((2, *plane), f32),
            pltpu.VMEM(plane, jnp.int32),
            pltpu.VMEM(now.shape, f32),
            pltpu.VMEM((3, 2, *plane), f32),
            pltpu.VMEM((4, 2, *plane), f32),
            pltpu.VMEM((2, *plane), jnp.bfloat16),
            pltpu.VMEM((2, *plane), jnp.bfloat16),
            pltpu.VMEM(now.shape, f32),
            pltpu.VMEM((8, 2, *plane), f32),
            pltpu.VMEM((7, 4, *plane), f32),
            pltpu.VMEM(plane, f32),
            pltpu.VMEM((lhs_rows, nrec), f32),
            pltpu.VMEM((lhs_rows, cols), f32),
            pltpu.VMEM(((tiles + 2) * group, cols), f32),
            pltpu.VMEM((2, tiles, group, cols), jnp.bfloat16),
            pltpu.VMEM((2, tiles, group, cols), jnp.bfloat16),
            pltpu.VMEM((2, LINES // rows * group, cols), f32),
            pltpu.VMEM((ngroups, NLAG, (per + 2) // 2, 2 * LINES, cols), f32),
            pltpu.VMEM((NLAG, per, LINES, cols), f32),
            pltpu.VMEM((NLAG, per, LINES, cols), f32),
            pltpu.VMEM((2 * NLAG, LINES * per, cols), f32),
            pltpu.SemaphoreType.DMA((4,)),
            pltpu.SemaphoreType.DMA((4,)),
            pltpu.SemaphoreType.DMA((6,)),
            pltpu.SemaphoreType.DMA((6,)),
            pltpu.SemaphoreType.DMA((2, tiles)),
            pltpu.SemaphoreType.DMA((2, tiles)),
            pltpu.SemaphoreType.DMA((10,)),
            pltpu.SemaphoreType.REGULAR((max(1, tiles.bit_length()),)),
        ],
        compiler_params=pltpu.CompilerParams(collective_id=0, has_side_effects=True),
    )(now, prev, facies, vel, eps, tilt, src_cell, wavelet, cells.reshape(1, nrec), data)
    filtered, wave = pl.pallas_call(
        stored,
        out_shape=(
            jax.ShapeDtypeStruct(filtered.shape, jnp.bfloat16),
            jax.ShapeDtypeStruct(now.shape, f32),
        ),
        in_specs=[vmem] * 2,
        out_specs=(hbm, hbm),
        scratch_shapes=[pltpu.SemaphoreType.DMA((2,))],
        compiler_params=pltpu.CompilerParams(vmem_limit_bytes=1 << 20),
    )(filtered, wave)
    return filtered.reshape(NLAG, rows * tiles, per, cols), wave


def solution(mesh):
    return jax.shard_map(
        functools.partial(shards, mesh.shape["tile"]),
        mesh=mesh,
        in_specs=(
            P("shot", "tile", None, None),
            P("shot", "tile", None, None),
            P("tile", None, None),
            P(),
            P(),
            P(),
            P("shot"),
            P("shot"),
            P("shot"),
            P(None, "shot"),
        ),
        out_specs=(P("shot", None, "tile", None), P("shot", "tile", None, None)),
        check_vma=False,
    )
```

```python
import functools

import jax
import jax.numpy as jnp
from jax import lax
from jax.experimental import pallas as pl
from jax.experimental.pallas import tpu as pltpu
from jax.sharding import PartitionSpec as P

NLAG = 32
STEPS = 4
REACH = 4
PARTS = 4
LINES = 8


def in_order(count, body):
    def run(i, carry):
        body(i)
        return carry

    lax.fori_loop(0, count, run, 0)


def kernel(
    tiles,
    now,
    prev_in,
    facies_in,
    vel_in,
    eps_in,
    tilt_in,
    src_in,
    wavelet_in,
    cells_in,
    data_in,
    out,
    wave_out,
    own,
    prev,
    facies,
    vel_tab,
    eps_tab,
    tilt_tab,
    src_cell,
    wavelet,
    cells,
    data,
    mate_now,
    mate_prev,
    mate_fac,
    mate_near,
    mate_edge,
    trace_send,
    trace_recv,
    fac_send,
    fac_recv,
    two,
    work,
    coef,
    far_two,
    lhs,
    surf,
    blocks,
    send,
    recv,
    staged,
    part_image,
    last_own,
    last_sum,
    woven,
    mate_send_sem,
    mate_recv_sem,
    far_send_sem,
    far_recv_sem,
    snap_send,
    snap_recv,
    load_sem,
    entered_sem,
    below_sem,
    above_sem,
):
    rows, depth, cols = facies.shape
    per = depth // tiles
    nrec = data.shape[1]
    group = 2 * rows * (per + 2)
    margin = NLAG // 2
    ngroups = tiles * rows // LINES
    members = LINES // rows
    pairs = (per + 2) // 2
    me = lax.axis_index("tile")
    odd = lax.rem(me, 2)
    even = 1 - odd
    mate = me + 1 - 2 * odd
    far = me - 1 + 2 * odd
    has_far = (far >= 0) & (far < tiles)

    reaches = []
    while (REACH << len(reaches)) < tiles - 1:
        reaches.append(REACH << len(reaches))

    barrier = pltpu.get_barrier_semaphore()

    def signal_at(semaphore, *ways):
        for way in ways:
            peer = me + way
            there = (peer >= 0) & (peer < tiles)

            @pl.when(there)
            def _():
                pl.semaphore_signal(semaphore, inc=1, device_id={"tile": peer})

    def tell(n):
        signal_at(below_sem.at[n], reaches[n])
        signal_at(above_sem.at[n], -reaches[n])

    def hear_below(n):
        @pl.when(me >= reaches[n])
        def _():
            pl.semaphore_wait(below_sem.at[n], 1)

    def hear_above(n):
        @pl.when(me + reaches[n] < tiles)
        def _():
            pl.semaphore_wait(above_sem.at[n], 1)

    reach = min(REACH, tiles - 1)
    signal_at(barrier, -1, 1)
    loads = [
        pltpu.make_async_copy(src, dst, load_sem.at[n])
        for n, (src, dst) in enumerate(
            (
                (now, own),
                (prev_in, prev),
                (facies_in, facies),
                (vel_in, vel_tab),
                (eps_in, eps_tab),
                (tilt_in, tilt_tab),
                (cells_in, cells),
                (data_in, data),
                (src_in, src_cell),
                (wavelet_in, wavelet),
            )
        )
    ]
    for load in loads:
        load.start()
    signal_at(barrier, *range(2, reach + 1))

    zero_plane = jnp.zeros((depth, cols), jnp.float32)

    @pl.when(jnp.logical_not(has_far))
    def _():
        for f in range(2):
            for k in range(STEPS):
                trace_recv[k, f] = zero_plane
        for n in range(2):
            fac_recv[n] = jnp.full((depth, cols), -1.0, jnp.bfloat16)

    def remote(src, dst, ssem, rsem, peer):
        return pltpu.make_async_remote_copy(
            src_ref=src, dst_ref=dst, send_sem=ssem, recv_sem=rsem, device_id={"tile": peer}
        )

    def mate_copy(n, src, dst):
        return remote(src, dst, mate_send_sem.at[n], mate_recv_sem.at[n], mate)

    def far_copy(n, src, dst):
        return remote(src, dst, far_send_sem.at[n], far_recv_sem.at[n], far)

    mate_first = (
        mate_copy(0, own, mate_now),
        mate_copy(1, prev.at[:, even], mate_prev),
        mate_copy(2, facies.at[even], mate_fac),
    )
    mate_second = mate_copy(3, two.at[:, even], mate_near)
    mate_third = mate_copy(4, two.at[:, odd], mate_edge)
    far_fac = far_copy(0, fac_send.at[0], fac_recv.at[0])
    far_deep = far_copy(1, fac_send.at[1], fac_recv.at[1])
    far_now = far_copy(2, own.at[:, odd], trace_recv.at[0])
    far_one, far_second, far_third = (
        far_copy(3 + k, trace_send.at[k], trace_recv.at[k + 1]) for k in range(3)
    )
    far_all = (far_fac, far_now, far_one, far_deep, far_second, far_third)

    def from_far(*copies):
        @pl.when(has_far)
        def _():
            for copy in copies:
                copy.wait_recv()

    def to_far(*copies):
        @pl.when(has_far)
        def _():
            for copy in copies:
                copy.start()

    lines = (me * rows + odd, me * rows + even, mate * rows + odd, far * rows + even)

    def looked_up(kinds):
        vel = jnp.zeros((depth, cols), jnp.float32)
        eps, tlt = vel, vel
        for n in range(vel_tab.shape[0]):
            here = kinds == n
            vel = jnp.where(here, vel_tab[n], vel)
            eps = jnp.where(here, eps_tab[n], eps)
            tlt = jnp.where(here, tilt_tab[n], tlt)
        return vel, vel * (1.0 + 2.0 * eps), 0.25 * vel * tlt

    lane = lax.broadcasted_iota(jnp.int32, (depth, cols), 1)
    level = lax.broadcasted_iota(jnp.int32, (depth, cols), 0)
    first_lane, last_lane = lane == 0, lane == cols - 1
    first_level, last_level = level == 0, level == depth - 1
    surface_lane = lax.broadcasted_iota(jnp.int32, (1, cols), 1)

    to_right = lambda v: pltpu.roll(v, 1, 1)
    to_left = lambda v: pltpu.roll(v, cols - 1, 1)

    def fill_coef(i, kinds):
        vel, flat, tlt = looked_up(kinds)
        coef[0, i] = 2.0 - 4.0 * flat - 2.0 * vel
        coef[1, i] = flat
        coef[2, i] = vel
        coef[3, i] = jnp.where(first_lane, 0.0, to_right(flat))
        coef[4, i] = jnp.where(first_lane, 0.0, to_right(tlt))
        coef[5, i] = jnp.where(last_lane, 0.0, to_left(flat))
        coef[6, i] = jnp.where(last_lane, 0.0, to_left(tlt))

    def advance(i, current, above, below, old):
        deeper = jnp.where(last_level, 0.0, pltpu.roll(current, depth - 1, 0))
        higher = jnp.where(first_level, 0.0, pltpu.roll(current, 1, 0))
        slope = deeper - higher
        new = to_left(coef[3, i] * current + coef[4, i] * slope)
        new = new + to_right(coef[5, i] * current - coef[6, i] * slope)
        new = new + coef[2, i] * (deeper + higher) + coef[0, i] * current
        if above is not None:
            new = new + coef[1, i] * (above if below is None else above + below)
        elif below is not None:
            new = new + coef[1, i] * below
        return new if old is None else new - old

    def inject(step, f, i, new):
        if f == 0:
            added = jnp.where(surface_lane == src_cell[0] - lines[i] * cols, wavelet[step], 0.0)
        else:
            at = i * PARTS * STEPS + step
            added = surf[at : at + 1, :]
            for p in range(1, 3):
                added = added + surf[at + p * STEPS : at + p * STEPS + 1, :]
        return new + jnp.where(first_level, added, 0.0)

    loads[0].wait()
    pl.semaphore_wait(barrier, jnp.minimum(me, reach) + jnp.minimum(tiles - 1 - me, 1))
    to_far(far_now)
    mate_first[0].start()
    for load in loads[1:6]:
        load.wait()
    for copy in mate_first[1:]:
        copy.start()
    fac_send[0] = facies[odd].astype(jnp.float32).astype(jnp.bfloat16)
    fac_send[1] = facies[even].astype(jnp.float32).astype(jnp.bfloat16)
    fill_coef(0, facies[odd])
    for f in range(2):
        trace_send[0, f] = advance(0, own[f, odd], None, own[f, even], prev[f, odd])
    to_far(far_fac, far_one, far_deep)

    signal_at(entered_sem.at[0], *range(-reach, -1))

    for load in loads[6:]:
        load.wait()

    cell = cells[...]
    column = cell & (cols - 1) if cols & (cols - 1) == 0 else lax.rem(cell, cols)
    onehot = (lax.broadcasted_iota(jnp.int32, (cols, nrec), 0) == column).astype(jnp.float32)
    onehot = onehot.astype(jnp.bfloat16)
    amounts = data[...]
    high = amounts.astype(jnp.bfloat16).astype(jnp.float32)
    rest = amounts - high
    middle = rest.astype(jnp.bfloat16).astype(jnp.float32)
    parts = (high, middle, rest - middle, jnp.zeros_like(high))
    for i in range(4):
        first = lines[i] * cols
        inside = (cell >= first) & (cell < first + cols)
        for p, part in enumerate(parts):
            at = (i * PARTS + p) * STEPS
            lhs[at : at + STEPS, :] = jnp.where(inside, part, 0.0)
    surf[...] = lax.dot_general(
        lhs[...].astype(jnp.bfloat16), onehot, (((1,), (1,)), ((), ())),
        preferred_element_type=jnp.float32,
    )

    for f in range(2):
        work[3, f] = inject(0, f, 0, trace_send[0, f])
    fill_coef(1, facies[even])
    blocks[group : 2 * group, :] = jnp.zeros((group, cols), jnp.float32)
    blocks[group * tiles : group * (tiles + 1), :] = jnp.zeros((group, cols), jnp.float32)
    zero_lines = jnp.zeros((per, LINES, cols), jnp.float32)
    for k in range(NLAG):
        last_own[k] = zero_lines
        last_sum[k] = zero_lines

    mate_first[0].wait_recv()
    for f in range(2):
        work[0, f] = inject(
            0, f, 1, advance(1, own[f, even], own[f, odd], mate_now[f, odd], prev[f, even])
        )
        trace_send[1, f] = inject(
            1, f, 0, advance(0, work[3, f], None, work[0, f], own[f, odd])
        )
    to_far(far_second)
    for copy in mate_first[1:]:
        copy.wait_recv()
    fill_coef(2, mate_fac[...])
    for f in range(2):
        work[1, f] = inject(
            0, f, 2, advance(2, mate_now[f, odd], own[f, even], mate_now[f, even], mate_prev[f])
        )
        near = inject(1, f, 1, advance(1, work[0, f], work[3, f], work[1, f], own[f, even]))
        work[2, f] = near
        trace_send[2, f] = inject(2, f, 0, advance(0, trace_send[1, f], None, near, work[3, f]))
    to_far(far_third)

    beyond_next = jnp.minimum(tiles - 2 - me, reach - 1)

    @pl.when(beyond_next > 0)
    def _():
        pl.semaphore_wait(entered_sem.at[0], beyond_next)

    if reaches:
        tell(0)

    from_far(far_fac)
    fill_coef(3, fac_recv[0].astype(jnp.float32))
    if len(reaches) > 1:
        hear_below(0)
        hear_above(0)
        tell(1)
    from_far(far_now)
    for f in range(2):
        push = coef[1, 0] * trace_recv[0, f]
        one = work[3, f] + push
        echo = coef[1, 3] * own[f, odd]
        two[f, even] = work[2, f] + coef[1, 1] * push
        new = advance(0, one, inject(0, f, 3, echo), work[0, f], own[f, odd])
        work[8, f] = inject(1, f, 0, new)
        work[3, f] = one
        work[4, f] = echo
    mate_second.start()
    from_far(far_one)
    for f in range(2):
        two[f, odd] = work[8, f] + coef[1, 0] * trace_recv[1, f]
    mate_third.start()

    def pack_snapshot(s, source):
        for r in range(rows):
            for f in range(2):
                at = (r * 2 + f) * (per + 2)
                upper = source[f, r, pl.ds(0, tiles, stride=2), :]
                lower = source[f, r, pl.ds(1, tiles, stride=2), :]
                blocks[pl.ds(at + 2 * group, tiles, stride=group), :] = lower
                blocks[pl.ds(at + group + 1, tiles, stride=group), :] = upper
                blocks[pl.ds(at + group + 2, tiles, stride=group), :] = lower
                blocks[pl.ds(at + 3, tiles, stride=group), :] = upper
        for d in range(tiles):
            at = (d + 1) * group
            send[s, d] = blocks[at : at + group, :].astype(jnp.bfloat16)
    def snap_copy(s, peer):
        return remote(
            send.at[s, peer], recv.at[s, me], snap_send.at[s, peer], snap_recv.at[s, me], peer
        )

    def other(peer, action):
        @pl.when(peer != me)
        def _():
            action(peer)

    def each_peer(action):
        in_order(tiles, lambda peer: other(peer, action))

    def send_to(s, first, end):
        def run(peer, carry):
            snap_copy(s, peer).start()
            return carry

        lax.fori_loop(first, end, run, 0)

    def send_below(s):
        send_to(s, 0, me)

    def send_above(s):
        send_to(s, me + 1, tiles)
        recv[s, me] = send[s, me]

    for n in range(1, len(reaches) - 1):
        hear_below(n)
        hear_above(n)
        tell(n + 1)
    if reaches:
        hear_below(len(reaches) - 1)
    pack_snapshot(0, two)
    send_below(0)

    from_far(far_deep)
    far_two[...] = looked_up(fac_recv[1].astype(jnp.float32))[1]
    for f in range(2):
        echo = work[4, f]
        echo_two = advance(3, echo, work[3, f], None, None)
        work[5, f] = advance(3, echo_two, two[f, odd], far_two[...] * echo, echo)
        new = advance(0, two[f, odd], echo_two, two[f, even], work[3, f])
        work[6, f] = inject(2, f, 0, new)

    mate_second.wait_recv()
    for f in range(2):
        new = advance(1, two[f, even], two[f, odd], mate_near[f], work[0, f])
        work[7, f] = inject(2, f, 1, new)
        new = advance(2, mate_near[f], two[f, even], None, work[1, f])
        work[8, f] = inject(2, f, 2, new)

    from_far(far_second)
    for f in range(2):
        edge = work[6, f] + coef[1, 0] * trace_recv[2, f]
        near = work[7, f]
        new = advance(0, edge, work[5, f], near, two[f, odd])
        wave_out[f, odd] = inject(3, f, 0, new)
        new = advance(1, near, edge, work[8, f], two[f, even])
        wave_out[f, even] = inject(3, f, 1, new)
    mate_third.wait_recv()
    for f in range(2):
        wave_out[f, even] = wave_out[f, even] + coef[1, 1] * (coef[1, 2] * mate_edge[f])
    from_far(far_third)
    for f in range(2):
        wave_out[f, odd] = wave_out[f, odd] + coef[1, 0] * trace_recv[3, f]
    pack_snapshot(1, wave_out)
    send_below(1)
    if reaches:
        hear_above(len(reaches) - 1)
    send_above(0)
    send_above(1)

    image_lane = lax.broadcasted_iota(jnp.int32, (1, cols), 1)
    line = lax.broadcasted_iota(jnp.int32, (LINES, cols), 0)
    last_line = line == LINES - 1

    def arrived(s, g):
        for i in range(members):
            peer = g * members + i

            @pl.when(peer != me)
            def _():
                remote(
                    send.at[s, me], recv.at[s, peer], snap_send.at[s, me], snap_recv.at[s, peer], peer
                ).wait_recv()

        for i in range(members):
            staged[s, i * group : (i + 1) * group, :] = recv[s, g * members + i].astype(jnp.float32)
        lifted = lambda f, j: staged[
            s, pl.ds(f * (per + 2) + j, LINES, stride=2 * (per + 2)), :
        ]
        return [
            [
                jnp.concatenate([lifted(f, j), lifted(f, j + 1)], axis=0)
                for j in range(0, per + 2, 2)
            ]
            for f in range(2)
        ]

    def turned(values, amount):
        amount = amount % cols
        return pltpu.roll(values, amount, 1) if amount else values

    def first_products(g):
        ahead, behind = arrived(0, g)
        behind = [v.astype(jnp.bfloat16) for v in behind]
        for k in range(NLAG):
            for j in range(pairs):
                pulled = turned(behind[j], 2 * (margin - k)).astype(jnp.float32)
                part_image[g, k, j] = ahead[j] * pulled

    def finish(g, last):
        ahead, behind = arrived(1, g)
        behind = [v.astype(jnp.bfloat16) for v in behind]

        def write(slot, h, at, results):
            for z in range(per):
                woven[slot, pl.ds(z, LINES, stride=per), :] = results[z]
            out[h + margin, at] = turned(woven[slot].astype(jnp.bfloat16), h)

        for k in range(NLAG):
            h = k - margin
            products = [
                part_image[g, k, j] + ahead[j] * turned(behind[j], -2 * h).astype(jnp.float32)
                for j in range(pairs)
            ]
            if h > 0:
                products = [jnp.where(image_lane < cols - 2 * h, v, 0.0) for v in products]
            elif h < 0:
                products = [jnp.where(image_lane >= -2 * h, v, 0.0) for v in products]
            image = jnp.concatenate(products, axis=0)
            image = image.astype(jnp.bfloat16).astype(jnp.float32)
            plane = [image[j * LINES : (j + 1) * LINES] for j in range(per + 2)]
            before, sums = [], []
            for z in range(per):
                mine = plane[z + 1]
                lower, higher = turned(mine, 1), turned(mine, -1)
                if h == 0:
                    lower = jnp.where(image_lane == 0, 0.0, lower)
                    higher = jnp.where(image_lane == cols - 1, 0.0, higher)
                total = (lower + higher) + (plane[z] + plane[z + 2])
                total = total + pltpu.roll(jnp.where(last_line, last_own[k, z], mine), 1, 0)
                later = pltpu.roll(mine, LINES - 1, 0)
                total = total + jnp.where(last_line, 0.0, later)
                before.append(0.125 * (last_sum[k, z] - jnp.where(last_line, later, 0.0)))
                sums.append(6.0 * mine - total)
            if last:
                if ngroups > 1:
                    write(2 * k, h, g - 1, before)
                write(2 * k + 1, h, g, [0.125 * value for value in sums])
            else:
                write(2 * k, h, jnp.maximum(g - 1, 0), before)
                for z in range(per):
                    last_own[k, z] = plane[z + 1]
                    last_sum[k, z] = sums[z]

    first_products(0)

    def both(g):
        first_products(g + 1)
        finish(g, False)

    in_order(ngroups - 1, both)
    for copy in mate_first:
        copy.wait_send()
    mate_second.wait_send()
    mate_third.wait_send()

    @pl.when(has_far)
    def _():
        for copy in far_all:
            copy.wait_send()

    for s in range(2):
        each_peer(lambda peer: snap_copy(s, peer).wait_send())

    finish(ngroups - 1, True)

def stored(filtered_in, wave_in, filtered, wave, sems):
    copies = [
        pltpu.make_async_copy(src, dst, sems.at[n])
        for n, (src, dst) in enumerate(((filtered_in, filtered), (wave_in, wave)))
    ]
    for copy in copies:
        copy.start()
    for copy in copies:
        copy.wait()


def shards(tiles, now, prev, facies, vel, eps, tilt, src_cell, wavelet, cells, data):
    rows, depth, cols = facies.shape
    per = depth // tiles
    nrec = cells.shape[0]
    group = 2 * rows * (per + 2)
    ngroups = tiles * rows // LINES
    assert rows == 2 and per == 2 and tiles * rows % LINES == 0
    f32 = jnp.float32
    vmem = pl.BlockSpec(memory_space=pltpu.VMEM)
    hbm = pl.BlockSpec(memory_space=pltpu.HBM)
    lhs_rows = 4 * PARTS * STEPS
    plane = (depth, cols)
    filtered, wave = pl.pallas_call(
        functools.partial(kernel, tiles),
        out_shape=(
            pltpu.VMEM((NLAG, ngroups, LINES * per, cols), jnp.bfloat16),
            pltpu.VMEM(now.shape, f32),
        ),
        in_specs=[hbm] * 10,
        out_specs=(vmem, vmem),
        scratch_shapes=[
            pltpu.VMEM(now.shape, f32),
            pltpu.VMEM(prev.shape, f32),
            pltpu.VMEM(facies.shape, jnp.int32),
            pltpu.SMEM(vel.shape, f32),
            pltpu.SMEM(eps.shape, f32),
            pltpu.SMEM(tilt.shape, f32),
            pltpu.SMEM(src_cell.shape, jnp.int32),
            pltpu.SMEM(wavelet.shape, f32),
            pltpu.VMEM((1, nrec), jnp.int32),
            pltpu.VMEM(data.shape, f32),
            pltpu.VMEM(now.shape, f32),
            pltpu.VMEM((2, *plane), f32),
            pltpu.VMEM(plane, jnp.int32),
            pltpu.VMEM((2, *plane), f32),
            pltpu.VMEM((2, *plane), f32),
            pltpu.VMEM((3, 2, *plane), f32),
            pltpu.VMEM((4, 2, *plane), f32),
            pltpu.VMEM((2, *plane), jnp.bfloat16),
            pltpu.VMEM((2, *plane), jnp.bfloat16),
            pltpu.VMEM(now.shape, f32),
            pltpu.VMEM((9, 2, *plane), f32),
            pltpu.VMEM((7, 4, *plane), f32),
            pltpu.VMEM(plane, f32),
            pltpu.VMEM((lhs_rows, nrec), f32),
            pltpu.VMEM((lhs_rows, cols), f32),
            pltpu.VMEM(((tiles + 2) * group, cols), f32),
            pltpu.VMEM((2, tiles, group, cols), jnp.bfloat16),
            pltpu.VMEM((2, tiles, group, cols), jnp.bfloat16),
            pltpu.VMEM((2, LINES // rows * group, cols), f32),
            pltpu.VMEM((ngroups, NLAG, (per + 2) // 2, 2 * LINES, cols), f32),
            pltpu.VMEM((NLAG, per, LINES, cols), f32),
            pltpu.VMEM((NLAG, per, LINES, cols), f32),
            pltpu.VMEM((2 * NLAG, LINES * per, cols), f32),
            pltpu.SemaphoreType.DMA((5,)),
            pltpu.SemaphoreType.DMA((5,)),
            pltpu.SemaphoreType.DMA((6,)),
            pltpu.SemaphoreType.DMA((6,)),
            pltpu.SemaphoreType.DMA((2, tiles)),
            pltpu.SemaphoreType.DMA((2, tiles)),
            pltpu.SemaphoreType.DMA((10,)),
            pltpu.SemaphoreType.REGULAR((1,)),
            pltpu.SemaphoreType.REGULAR((max(1, tiles.bit_length()),)),
            pltpu.SemaphoreType.REGULAR((max(1, tiles.bit_length()),)),
        ],
        compiler_params=pltpu.CompilerParams(collective_id=0, has_side_effects=True),
    )(now, prev, facies, vel, eps, tilt, src_cell, wavelet, cells.reshape(1, nrec), data)
    filtered, wave = pl.pallas_call(
        stored,
        out_shape=(
            jax.ShapeDtypeStruct(filtered.shape, jnp.bfloat16),
            jax.ShapeDtypeStruct(now.shape, f32),
        ),
        in_specs=[vmem] * 2,
        out_specs=(hbm, hbm),
        scratch_shapes=[pltpu.SemaphoreType.DMA((2,))],
        compiler_params=pltpu.CompilerParams(vmem_limit_bytes=1 << 20),
    )(filtered, wave)
    return filtered.reshape(NLAG, rows * tiles, per, cols), wave


def solution(mesh):
    return jax.shard_map(
        functools.partial(shards, mesh.shape["tile"]),
        mesh=mesh,
        in_specs=(
            P("shot", "tile", None, None),
            P("shot", "tile", None, None),
            P("tile", None, None),
            P(),
            P(),
            P(),
            P("shot"),
            P("shot"),
            P("shot"),
            P(None, "shot"),
        ),
        out_specs=(P("shot", None, "tile", None), P("shot", "tile", None, None)),
        check_vma=False,
    )
```

```python
import functools

import jax
import jax.numpy as jnp
from jax import lax
from jax.experimental import pallas as pl
from jax.experimental.pallas import tpu as pltpu
from jax.sharding import PartitionSpec as P

NLAG = 32
STEPS = 4
REACH = 4
PARTS = 4
LINES = 8


def in_order(count, body):
    def run(i, carry):
        body(i)
        return carry

    lax.fori_loop(0, count, run, 0)


def kernel(
    tiles,
    now,
    prev_in,
    facies_in,
    vel_in,
    eps_in,
    tilt_in,
    src_in,
    wavelet_in,
    cells_in,
    data_in,
    out,
    wave_out,
    own,
    prev,
    facies,
    vel_tab,
    eps_tab,
    tilt_tab,
    src_cell,
    wavelet,
    cells,
    data,
    mate_now,
    mate_prev,
    mate_fac,
    mate_near,
    mate_edge,
    trace_send,
    trace_recv,
    fac_send,
    fac_recv,
    two,
    work,
    coef,
    far_two,
    lhs,
    surf,
    blocks,
    send,
    recv,
    staged,
    part_image,
    last_own,
    last_sum,
    woven,
    mate_send_sem,
    mate_recv_sem,
    far_send_sem,
    far_recv_sem,
    snap_send,
    snap_recv,
    load_sem,
    entered_sem,
    below_sem,
    above_sem,
):
    rows, depth, cols = facies.shape
    per = depth // tiles
    nrec = data.shape[1]
    group = 2 * rows * (per + 2)
    margin = NLAG // 2
    ngroups = tiles * rows // LINES
    members = LINES // rows
    pairs = (per + 2) // 2
    me = lax.axis_index("tile")
    odd = lax.rem(me, 2)
    even = 1 - odd
    mate = me + 1 - 2 * odd
    far = me - 1 + 2 * odd
    has_far = (far >= 0) & (far < tiles)

    reaches = []
    while (REACH << len(reaches)) < tiles - 1:
        reaches.append(REACH << len(reaches))

    barrier = pltpu.get_barrier_semaphore()

    def signal_at(semaphore, *ways):
        for way in ways:
            peer = me + way
            there = (peer >= 0) & (peer < tiles)

            @pl.when(there)
            def _():
                pl.semaphore_signal(semaphore, inc=1, device_id={"tile": peer})

    def tell(n):
        signal_at(below_sem.at[n], reaches[n])
        signal_at(above_sem.at[n], -reaches[n])

    def hear_below(n):
        @pl.when(me >= reaches[n])
        def _():
            pl.semaphore_wait(below_sem.at[n], 1)

    def hear_above(n):
        @pl.when(me + reaches[n] < tiles)
        def _():
            pl.semaphore_wait(above_sem.at[n], 1)

    reach = min(REACH, tiles - 1)
    signal_at(barrier, -1, 1)
    loads = [
        pltpu.make_async_copy(src, dst, load_sem.at[n])
        for n, (src, dst) in enumerate(
            (
                (now, own),
                (prev_in, prev),
                (facies_in, facies),
                (vel_in, vel_tab),
                (eps_in, eps_tab),
                (tilt_in, tilt_tab),
                (cells_in, cells),
                (data_in, data),
                (src_in, src_cell),
                (wavelet_in, wavelet),
            )
        )
    ]
    for load in loads:
        load.start()
    signal_at(barrier, *range(2, reach + 1))

    zero_plane = jnp.zeros((depth, cols), jnp.float32)

    @pl.when(jnp.logical_not(has_far))
    def _():
        for f in range(2):
            for k in range(STEPS):
                trace_recv[k, f] = zero_plane
        for n in range(2):
            fac_recv[n] = jnp.full((depth, cols), -1.0, jnp.bfloat16)

    def remote(src, dst, ssem, rsem, peer):
        return pltpu.make_async_remote_copy(
            src_ref=src, dst_ref=dst, send_sem=ssem, recv_sem=rsem, device_id={"tile": peer}
        )

    def mate_copy(n, src, dst):
        return remote(src, dst, mate_send_sem.at[n], mate_recv_sem.at[n], mate)

    def far_copy(n, src, dst):
        return remote(src, dst, far_send_sem.at[n], far_recv_sem.at[n], far)

    mate_first = (
        mate_copy(0, own, mate_now),
        mate_copy(1, prev.at[:, even], mate_prev),
        mate_copy(2, facies.at[even], mate_fac),
    )
    mate_second = mate_copy(3, two.at[:, even], mate_near)
    mate_third = mate_copy(4, two.at[:, odd], mate_edge)
    far_fac = far_copy(0, fac_send.at[0], fac_recv.at[0])
    far_deep = far_copy(1, fac_send.at[1], fac_recv.at[1])
    far_now = far_copy(2, own.at[:, odd], trace_recv.at[0])
    far_one, far_second, far_third = (
        far_copy(3 + k, trace_send.at[k], trace_recv.at[k + 1]) for k in range(3)
    )
    far_all = (far_fac, far_now, far_one, far_deep, far_second, far_third)

    def from_far(*copies):
        @pl.when(has_far)
        def _():
            for copy in copies:
                copy.wait_recv()

    def to_far(*copies):
        @pl.when(has_far)
        def _():
            for copy in copies:
                copy.start()

    lines = (me * rows + odd, me * rows + even, mate * rows + odd, far * rows + even)

    def looked_up(kinds):
        vel = jnp.zeros((depth, cols), jnp.float32)
        eps, tlt = vel, vel
        for n in range(vel_tab.shape[0]):
            here = kinds == n
            vel = jnp.where(here, vel_tab[n], vel)
            eps = jnp.where(here, eps_tab[n], eps)
            tlt = jnp.where(here, tilt_tab[n], tlt)
        return vel, vel * (1.0 + 2.0 * eps), 0.25 * vel * tlt

    lane = lax.broadcasted_iota(jnp.int32, (depth, cols), 1)
    level = lax.broadcasted_iota(jnp.int32, (depth, cols), 0)
    first_lane, last_lane = lane == 0, lane == cols - 1
    first_level, last_level = level == 0, level == depth - 1
    surface_lane = lax.broadcasted_iota(jnp.int32, (1, cols), 1)

    to_right = lambda v: pltpu.roll(v, 1, 1)
    to_left = lambda v: pltpu.roll(v, cols - 1, 1)

    def fill_coef(i, kinds):
        vel, flat, tlt = looked_up(kinds)
        coef[0, i] = 2.0 - 4.0 * flat - 2.0 * vel
        coef[1, i] = flat
        coef[2, i] = vel
        coef[3, i] = jnp.where(first_lane, 0.0, to_right(flat))
        coef[4, i] = jnp.where(first_lane, 0.0, to_right(tlt))
        coef[5, i] = jnp.where(last_lane, 0.0, to_left(flat))
        coef[6, i] = jnp.where(last_lane, 0.0, to_left(tlt))

    def advance(i, current, above, below, old):
        deeper = jnp.where(last_level, 0.0, pltpu.roll(current, depth - 1, 0))
        higher = jnp.where(first_level, 0.0, pltpu.roll(current, 1, 0))
        slope = deeper - higher
        new = to_left(coef[3, i] * current + coef[4, i] * slope)
        new = new + to_right(coef[5, i] * current - coef[6, i] * slope)
        new = new + coef[2, i] * (deeper + higher) + coef[0, i] * current
        if above is not None:
            new = new + coef[1, i] * (above if below is None else above + below)
        elif below is not None:
            new = new + coef[1, i] * below
        return new if old is None else new - old

    def inject(step, f, i, new):
        if f == 0:
            added = jnp.where(surface_lane == src_cell[0] - lines[i] * cols, wavelet[step], 0.0)
        else:
            at = i * PARTS * STEPS + step
            added = surf[at : at + 1, :]
            for p in range(1, 3):
                added = added + surf[at + p * STEPS : at + p * STEPS + 1, :]
        return new + jnp.where(first_level, added, 0.0)

    loads[0].wait()
    pl.semaphore_wait(barrier, jnp.minimum(me, reach) + jnp.minimum(tiles - 1 - me, 1))
    to_far(far_now)
    mate_first[0].start()
    for load in loads[1:6]:
        load.wait()
    for copy in mate_first[1:]:
        copy.start()
    fac_send[0] = facies[odd].astype(jnp.float32).astype(jnp.bfloat16)
    fac_send[1] = facies[even].astype(jnp.float32).astype(jnp.bfloat16)
    fill_coef(0, facies[odd])
    for f in range(2):
        trace_send[0, f] = advance(0, own[f, odd], None, own[f, even], prev[f, odd])
    to_far(far_fac, far_one, far_deep)

    signal_at(entered_sem.at[0], *range(-reach, -1))

    for load in loads[6:]:
        load.wait()

    cell = cells[...]
    column = cell & (cols - 1) if cols & (cols - 1) == 0 else lax.rem(cell, cols)
    onehot = (lax.broadcasted_iota(jnp.int32, (cols, nrec), 0) == column).astype(jnp.float32)
    onehot = onehot.astype(jnp.bfloat16)
    amounts = data[...]
    high = amounts.astype(jnp.bfloat16).astype(jnp.float32)
    rest = amounts - high
    middle = rest.astype(jnp.bfloat16).astype(jnp.float32)
    parts = (high, middle, rest - middle, jnp.zeros_like(high))
    for i in range(4):
        first = lines[i] * cols
        inside = (cell >= first) & (cell < first + cols)
        for p, part in enumerate(parts):
            at = (i * PARTS + p) * STEPS
            lhs[at : at + STEPS, :] = jnp.where(inside, part, 0.0)
    surf[...] = lax.dot_general(
        lhs[...].astype(jnp.bfloat16), onehot, (((1,), (1,)), ((), ())),
        preferred_element_type=jnp.float32,
    )

    for f in range(2):
        work[3, f] = inject(0, f, 0, trace_send[0, f])
    fill_coef(1, facies[even])
    blocks[group : 2 * group, :] = jnp.zeros((group, cols), jnp.float32)
    blocks[group * tiles : group * (tiles + 1), :] = jnp.zeros((group, cols), jnp.float32)
    zero_lines = jnp.zeros((per, LINES, cols), jnp.float32)
    for k in range(NLAG):
        last_own[k] = zero_lines
        last_sum[k] = zero_lines

    mate_first[0].wait_recv()
    for f in range(2):
        work[0, f] = inject(
            0, f, 1, advance(1, own[f, even], own[f, odd], mate_now[f, odd], prev[f, even])
        )
        trace_send[1, f] = inject(
            1, f, 0, advance(0, work[3, f], None, work[0, f], own[f, odd])
        )
    to_far(far_second)
    beyond_next = jnp.minimum(tiles - 2 - me, reach - 1)

    @pl.when(beyond_next > 0)
    def _():
        pl.semaphore_wait(entered_sem.at[0], beyond_next)

    if reaches:
        tell(0)
    for copy in mate_first[1:]:
        copy.wait_recv()
    fill_coef(2, mate_fac[...])
    for f in range(2):
        work[1, f] = inject(
            0, f, 2, advance(2, mate_now[f, odd], own[f, even], mate_now[f, even], mate_prev[f])
        )
        near = inject(1, f, 1, advance(1, work[0, f], work[3, f], work[1, f], own[f, even]))
        work[2, f] = near
        trace_send[2, f] = inject(2, f, 0, advance(0, trace_send[1, f], None, near, work[3, f]))
    to_far(far_third)


    if len(reaches) > 1:
        hear_below(0)
        hear_above(0)
        tell(1)
    from_far(far_fac)
    fill_coef(3, fac_recv[0].astype(jnp.float32))
    from_far(far_now)
    for f in range(2):
        push = coef[1, 0] * trace_recv[0, f]
        one = work[3, f] + push
        echo = coef[1, 3] * own[f, odd]
        two[f, even] = work[2, f] + coef[1, 1] * push
        new = advance(0, one, inject(0, f, 3, echo), work[0, f], own[f, odd])
        work[8, f] = inject(1, f, 0, new)
        work[3, f] = one
        work[4, f] = echo
    mate_second.start()
    from_far(far_one)
    for f in range(2):
        two[f, odd] = work[8, f] + coef[1, 0] * trace_recv[1, f]
    mate_third.start()

    def pack_snapshot(s, source):
        for r in range(rows):
            for f in range(2):
                at = (r * 2 + f) * (per + 2)
                upper = source[f, r, pl.ds(0, tiles, stride=2), :]
                lower = source[f, r, pl.ds(1, tiles, stride=2), :]
                blocks[pl.ds(at + 2 * group, tiles, stride=group), :] = lower
                blocks[pl.ds(at + group + 1, tiles, stride=group), :] = upper
                blocks[pl.ds(at + group + 2, tiles, stride=group), :] = lower
                blocks[pl.ds(at + 3, tiles, stride=group), :] = upper
        for d in range(tiles):
            at = (d + 1) * group
            send[s, d] = blocks[at : at + group, :].astype(jnp.bfloat16)
    def snap_copy(s, peer):
        return remote(
            send.at[s, peer], recv.at[s, me], snap_send.at[s, peer], snap_recv.at[s, me], peer
        )

    def other(peer, action):
        @pl.when(peer != me)
        def _():
            action(peer)

    def each_peer(action):
        in_order(tiles, lambda peer: other(peer, action))

    def send_to(s, first, end):
        def run(peer, carry):
            snap_copy(s, peer).start()
            return carry

        lax.fori_loop(first, end, run, 0)

    def send_below(s):
        send_to(s, 0, me)

    def send_above(s):
        send_to(s, me + 1, tiles)
        recv[s, me] = send[s, me]

    for n in range(1, len(reaches) - 1):
        hear_below(n)
        hear_above(n)
        tell(n + 1)
    if reaches:
        hear_below(len(reaches) - 1)
    pack_snapshot(0, two)
    send_below(0)

    from_far(far_deep)
    far_two[...] = looked_up(fac_recv[1].astype(jnp.float32))[1]
    for f in range(2):
        echo = work[4, f]
        echo_two = advance(3, echo, work[3, f], None, None)
        work[5, f] = advance(3, echo_two, two[f, odd], far_two[...] * echo, echo)
        new = advance(0, two[f, odd], echo_two, two[f, even], work[3, f])
        work[6, f] = inject(2, f, 0, new)

    mate_second.wait_recv()
    for f in range(2):
        new = advance(1, two[f, even], two[f, odd], mate_near[f], work[0, f])
        work[7, f] = inject(2, f, 1, new)
        new = advance(2, mate_near[f], two[f, even], None, work[1, f])
        work[8, f] = inject(2, f, 2, new)

    from_far(far_second)
    for f in range(2):
        edge = work[6, f] + coef[1, 0] * trace_recv[2, f]
        near = work[7, f]
        new = advance(0, edge, work[5, f], near, two[f, odd])
        wave_out[f, odd] = inject(3, f, 0, new)
        new = advance(1, near, edge, work[8, f], two[f, even])
        wave_out[f, even] = inject(3, f, 1, new)
    mate_third.wait_recv()
    for f in range(2):
        wave_out[f, even] = wave_out[f, even] + coef[1, 1] * (coef[1, 2] * mate_edge[f])
    from_far(far_third)
    for f in range(2):
        wave_out[f, odd] = wave_out[f, odd] + coef[1, 0] * trace_recv[3, f]
    pack_snapshot(1, wave_out)
    send_below(1)
    if reaches:
        hear_above(len(reaches) - 1)
    send_above(0)
    send_above(1)

    image_lane = lax.broadcasted_iota(jnp.int32, (1, cols), 1)
    line = lax.broadcasted_iota(jnp.int32, (LINES, cols), 0)
    last_line = line == LINES - 1

    def arrived(s, g):
        for i in range(members):
            peer = g * members + i

            @pl.when(peer != me)
            def _():
                remote(
                    send.at[s, me], recv.at[s, peer], snap_send.at[s, me], snap_recv.at[s, peer], peer
                ).wait_recv()

        for i in range(members):
            staged[s, i * group : (i + 1) * group, :] = recv[s, g * members + i].astype(jnp.float32)
        lifted = lambda f, j: staged[
            s, pl.ds(f * (per + 2) + j, LINES, stride=2 * (per + 2)), :
        ]
        return [
            [
                jnp.concatenate([lifted(f, j), lifted(f, j + 1)], axis=0)
                for j in range(0, per + 2, 2)
            ]
            for f in range(2)
        ]

    def turned(values, amount):
        amount = amount % cols
        return pltpu.roll(values, amount, 1) if amount else values

    def first_products(g):
        ahead, behind = arrived(0, g)
        behind = [v.astype(jnp.bfloat16) for v in behind]
        for k in range(NLAG):
            for j in range(pairs):
                pulled = turned(behind[j], 2 * (margin - k)).astype(jnp.float32)
                part_image[g, k, j] = ahead[j] * pulled

    def finish(g, last):
        ahead, behind = arrived(1, g)
        behind = [v.astype(jnp.bfloat16) for v in behind]

        def write(slot, h, at, results):
            for z in range(per):
                woven[slot, pl.ds(z, LINES, stride=per), :] = results[z]
            out[h + margin, at] = turned(woven[slot].astype(jnp.bfloat16), h)

        for k in range(NLAG):
            h = k - margin
            products = [
                part_image[g, k, j] + ahead[j] * turned(behind[j], -2 * h).astype(jnp.float32)
                for j in range(pairs)
            ]
            if h > 0:
                products = [jnp.where(image_lane < cols - 2 * h, v, 0.0) for v in products]
            elif h < 0:
                products = [jnp.where(image_lane >= -2 * h, v, 0.0) for v in products]
            image = jnp.concatenate(products, axis=0)
            image = image.astype(jnp.bfloat16).astype(jnp.float32)
            plane = [image[j * LINES : (j + 1) * LINES] for j in range(per + 2)]
            before, sums = [], []
            for z in range(per):
                mine = plane[z + 1]
                lower, higher = turned(mine, 1), turned(mine, -1)
                if h == 0:
                    lower = jnp.where(image_lane == 0, 0.0, lower)
                    higher = jnp.where(image_lane == cols - 1, 0.0, higher)
                total = (lower + higher) + (plane[z] + plane[z + 2])
                total = total + pltpu.roll(jnp.where(last_line, last_own[k, z], mine), 1, 0)
                later = pltpu.roll(mine, LINES - 1, 0)
                total = total + jnp.where(last_line, 0.0, later)
                before.append(0.125 * (last_sum[k, z] - jnp.where(last_line, later, 0.0)))
                sums.append(6.0 * mine - total)
            if last:
                if ngroups > 1:
                    write(2 * k, h, g - 1, before)
                write(2 * k + 1, h, g, [0.125 * value for value in sums])
            else:
                write(2 * k, h, jnp.maximum(g - 1, 0), before)
                for z in range(per):
                    last_own[k, z] = plane[z + 1]
                    last_sum[k, z] = sums[z]

    first_products(0)

    def both(g):
        first_products(g + 1)
        finish(g, False)

    in_order(ngroups - 1, both)
    for copy in mate_first:
        copy.wait_send()
    mate_second.wait_send()
    mate_third.wait_send()

    @pl.when(has_far)
    def _():
        for copy in far_all:
            copy.wait_send()

    for s in range(2):
        each_peer(lambda peer: snap_copy(s, peer).wait_send())

    finish(ngroups - 1, True)

def stored(filtered_in, wave_in, filtered, wave, sems):
    copies = [
        pltpu.make_async_copy(src, dst, sems.at[n])
        for n, (src, dst) in enumerate(((filtered_in, filtered), (wave_in, wave)))
    ]
    for copy in copies:
        copy.start()
    for copy in copies:
        copy.wait()


def shards(tiles, now, prev, facies, vel, eps, tilt, src_cell, wavelet, cells, data):
    rows, depth, cols = facies.shape
    per = depth // tiles
    nrec = cells.shape[0]
    group = 2 * rows * (per + 2)
    ngroups = tiles * rows // LINES
    assert rows == 2 and per == 2 and tiles * rows % LINES == 0
    f32 = jnp.float32
    vmem = pl.BlockSpec(memory_space=pltpu.VMEM)
    hbm = pl.BlockSpec(memory_space=pltpu.HBM)
    lhs_rows = 4 * PARTS * STEPS
    plane = (depth, cols)
    filtered, wave = pl.pallas_call(
        functools.partial(kernel, tiles),
        out_shape=(
            pltpu.VMEM((NLAG, ngroups, LINES * per, cols), jnp.bfloat16),
            pltpu.VMEM(now.shape, f32),
        ),
        in_specs=[hbm] * 10,
        out_specs=(vmem, vmem),
        scratch_shapes=[
            pltpu.VMEM(now.shape, f32),
            pltpu.VMEM(prev.shape, f32),
            pltpu.VMEM(facies.shape, jnp.int32),
            pltpu.SMEM(vel.shape, f32),
            pltpu.SMEM(eps.shape, f32),
            pltpu.SMEM(tilt.shape, f32),
            pltpu.SMEM(src_cell.shape, jnp.int32),
            pltpu.SMEM(wavelet.shape, f32),
            pltpu.VMEM((1, nrec), jnp.int32),
            pltpu.VMEM(data.shape, f32),
            pltpu.VMEM(now.shape, f32),
            pltpu.VMEM((2, *plane), f32),
            pltpu.VMEM(plane, jnp.int32),
            pltpu.VMEM((2, *plane), f32),
            pltpu.VMEM((2, *plane), f32),
            pltpu.VMEM((3, 2, *plane), f32),
            pltpu.VMEM((4, 2, *plane), f32),
            pltpu.VMEM((2, *plane), jnp.bfloat16),
            pltpu.VMEM((2, *plane), jnp.bfloat16),
            pltpu.VMEM(now.shape, f32),
            pltpu.VMEM((9, 2, *plane), f32),
            pltpu.VMEM((7, 4, *plane), f32),
            pltpu.VMEM(plane, f32),
            pltpu.VMEM((lhs_rows, nrec), f32),
            pltpu.VMEM((lhs_rows, cols), f32),
            pltpu.VMEM(((tiles + 2) * group, cols), f32),
            pltpu.VMEM((2, tiles, group, cols), jnp.bfloat16),
            pltpu.VMEM((2, tiles, group, cols), jnp.bfloat16),
            pltpu.VMEM((2, LINES // rows * group, cols), f32),
            pltpu.VMEM((ngroups, NLAG, (per + 2) // 2, 2 * LINES, cols), f32),
            pltpu.VMEM((NLAG, per, LINES, cols), f32),
            pltpu.VMEM((NLAG, per, LINES, cols), f32),
            pltpu.VMEM((2 * NLAG, LINES * per, cols), f32),
            pltpu.SemaphoreType.DMA((5,)),
            pltpu.SemaphoreType.DMA((5,)),
            pltpu.SemaphoreType.DMA((6,)),
            pltpu.SemaphoreType.DMA((6,)),
            pltpu.SemaphoreType.DMA((2, tiles)),
            pltpu.SemaphoreType.DMA((2, tiles)),
            pltpu.SemaphoreType.DMA((10,)),
            pltpu.SemaphoreType.REGULAR((1,)),
            pltpu.SemaphoreType.REGULAR((max(1, tiles.bit_length()),)),
            pltpu.SemaphoreType.REGULAR((max(1, tiles.bit_length()),)),
        ],
        compiler_params=pltpu.CompilerParams(collective_id=0, has_side_effects=True),
    )(now, prev, facies, vel, eps, tilt, src_cell, wavelet, cells.reshape(1, nrec), data)
    filtered, wave = pl.pallas_call(
        stored,
        out_shape=(
            jax.ShapeDtypeStruct(filtered.shape, jnp.bfloat16),
            jax.ShapeDtypeStruct(now.shape, f32),
        ),
        in_specs=[vmem] * 2,
        out_specs=(hbm, hbm),
        scratch_shapes=[pltpu.SemaphoreType.DMA((2,))],
        compiler_params=pltpu.CompilerParams(vmem_limit_bytes=1 << 20),
    )(filtered, wave)
    return filtered.reshape(NLAG, rows * tiles, per, cols), wave


def solution(mesh):
    return jax.shard_map(
        functools.partial(shards, mesh.shape["tile"]),
        mesh=mesh,
        in_specs=(
            P("shot", "tile", None, None),
            P("shot", "tile", None, None),
            P("tile", None, None),
            P(),
            P(),
            P(),
            P("shot"),
            P("shot"),
            P("shot"),
            P(None, "shot"),
        ),
        out_specs=(P("shot", None, "tile", None), P("shot", "tile", None, None)),
        check_vma=False,
    )
```
